512 devices in a mesh: dp: 512 (over z, x, y, core).
Axes of the slice: x: 4, y: 4, z: 16, core: 2. Of those that a mesh axis runs over, the one named last changes fastest.
Arguments:
- inputs: bfloat16 [2048, 199, 512], P('dp'), may hold values from -6 to 6
- weights: bfloat16 [2, 262144], replicated, may hold values from -0.1875 to 0.1875
- ln_gain: float32 [512], replicated, may hold values from 0.45 to 2.16
- ln_bias: float32 [512], replicated, may hold values from -3 to 3
- projection: bfloat16 [512, 1024], replicated, may hold values from -0.25 to 0.25
- targets: float32 [2048, 1024], P('dp'), may hold values from -6 to 6
- master: float32 [2, 262144], P(None, 'dp'), may hold values from -0.006 to 0.006
- first_moment: float32 [2, 262144], P(None, 'dp'), may hold values from -0.0006 to 0.0006
- second_moment: float32 [2, 262144], P(None, 'dp'), may hold values from 1e-11 to 1e-08
Outputs:
- input_grad: bfloat16 [2048, 199, 512], P('dp')
- update: float32 [2, 262144], P(None, 'dp')
- new_master: float32 [2, 262144], P(None, 'dp')
- new_first: float32 [2, 262144], P(None, 'dp')
- new_second: float32 [2, 262144], P(None, 'dp')
- new_weights: bfloat16 [2, 262144], replicated
The draws below stay inside these ranges and needn't reach their ends.
All inputs are finite; a program needn't handle non-finite values.
Results may differ from the reference program's by a relative error of at most 0.006.
Values may be sent and summed in bfloat16 or wider, within the bound.
No kernel may reach another device: no remote copies, remote signals or barrier semaphores. Data moves between devices by JAX's collectives and lax.ppermute only.
A program may use at most 64 MiB of HBM per device.

```python
import math
import jax
import jax.numpy as jnp
from jax import lax

C = 512
E = 1024
KW = 2
FIN = 199
CLIPS = 4
BATCH = 2048
N_DP = 512


def draw_ln_gain(key, part):
    inner = jax.random.fold_in(key, 11)
    ramp = 0.6 + 1.2 * jnp.arange(C, dtype=jnp.float32) / (C - 1)
    jitter = jax.random.uniform(inner, (C,), jnp.float32, 0.8, 1.2)
    return ramp * jitter


def shard_levels(own_key, extent, shards, low, top_value):
    loudness, own = 1.0, jax.random.fold_in(own_key, 6)
    for dim, shards_of in shards:
        heights = jnp.exp(jax.random.uniform(jax.random.fold_in(own, dim), (shards_of,), jnp.float32, low / len(shards), top_value / len(shards)))
        loudness = loudness * jnp.repeat(heights, extent[dim] // shards_of).reshape([-1 if axis == dim else 1 for axis in range(len(extent))])
    return loudness


def bell_draw(key, shape, deviation, reach, split=(), held_as=jnp.bfloat16):
    level = shard_levels(key, shape, split, -0.22, 0.18) if split else 1.0
    entries = jax.random.normal(key, shape, jnp.float32) * deviation * level
    return jnp.minimum(jnp.maximum(entries, -reach), reach).astype(held_as)


def setup_inputs(seed: int = 0) -> dict:
    seeds = jax.random.split(jax.random.key(seed), 10)
    inputs = bell_draw(seeds[0], (BATCH, FIN, C), 1.0, 6.0, ((0, 512),))
    weights = bell_draw(seeds[1], (KW, C * C), (KW * C) ** -0.5, 0.1875)
    ln_gain = draw_ln_gain(jax.random.fold_in(seeds[9], 71), 0)
    ln_bias = bell_draw(seeds[3], (C,), 0.5, 3.0, (), jnp.float32)
    projection = bell_draw(seeds[4], (C, E), C ** -0.5, 0.25)
    targets = bell_draw(seeds[5], (BATCH, E), 1.0, 6.0, ((0, 512),), jnp.float32)
    master = bell_draw(seeds[6], (KW, C * C), 0.001, 0.006, ((1, 512),), jnp.float32)
    first_moment = bell_draw(seeds[7], (KW, C * C), 0.0001, 0.0006, ((1, 512),), jnp.float32)
    second_moment = jnp.clip(jnp.exp(math.log(9.99999993922529e-09) - 6.9077553 * jax.random.uniform(seeds[8], (KW, C * C), jnp.float32) ** shard_levels(seeds[8], (KW, C * C), ((1, 512),), -0.2, 0.2)), 9.999999960041972e-12, 9.99999993922529e-09)
    return {"inputs": inputs, "weights": weights, "ln_gain": ln_gain, "ln_bias": ln_bias, "projection": projection, "targets": targets, "master": master, "first_moment": first_moment, "second_moment": second_moment}


def norm_act(pre, gain, bias):
    center = pre - lax.optimization_barrier(jnp.mean(pre, axis=-1, keepdims=True))
    spread = lax.optimization_barrier(jnp.mean(center * center, axis=-1, keepdims=True))
    normed = center * lax.rsqrt(spread + 1e-05)
    return jax.nn.gelu(normed * gain + bias, approximate=False)

def local_pass(inputs, weights, ln_gain, ln_bias, projection, targets):
    clips, frames_in, chans = inputs.shape
    taps = weights.shape[0]
    frames_out = (frames_in - taps) // taps + 1
    windows = inputs[:, :frames_out * taps].reshape(clips, frames_out, taps, chans)
    kernel = weights.reshape(taps, chans, chans)
    pre = jnp.einsum('bfki,koi->bfo', windows.astype(jnp.float32), kernel.astype(jnp.float32))
    act, pull = jax.vjp(lambda value: norm_act(value, ln_gain, ln_bias), pre)
    pooled = lax.optimization_barrier(jnp.mean(act, axis=1)).astype(jnp.bfloat16)
    predicted = jnp.dot(pooled, projection, preferred_element_type=jnp.float32)
    miss = (predicted - targets).astype(jnp.bfloat16)
    back = jnp.dot(miss, projection.T, preferred_element_type=jnp.float32)
    upstream = jnp.broadcast_to(back[:, None, :] / frames_out, act.shape)
    dpre = pull(upstream)[0].astype(jnp.bfloat16)
    dwin = jnp.einsum('bfo,koi->bfki', dpre.astype(jnp.float32), kernel.astype(jnp.float32)).astype(jnp.bfloat16)
    dinput = dwin.reshape(clips, frames_out * taps, chans)
    tail = jnp.zeros((clips, frames_in - frames_out * taps, chans), jnp.bfloat16)
    return (windows, dpre, jnp.concatenate([dinput, tail], axis=1))

def reference(inputs, weights, ln_gain, ln_bias, projection, targets, master, first_moment, second_moment):
    groups = inputs.reshape(N_DP, CLIPS, FIN, C)
    goals = targets.reshape(N_DP, CLIPS, E)

    def one_group(total, pair):
        windows, dpre, dinput = local_pass(pair[0], weights, ln_gain, ln_bias, projection, pair[1])
        term = jnp.einsum('bfo,bfki->koi', dpre.astype(jnp.float32), windows.astype(jnp.float32))
        return (total + term, dinput)
    start = jnp.zeros((KW, C, C), jnp.float32)
    grad, dinputs = lax.scan(one_group, start, (groups, goals))
    grad = grad.reshape(KW, C * C)
    norm_total = jnp.sqrt(jnp.sum(grad * grad))
    scale = jnp.minimum(1.0, 1.0 / (norm_total + 1e-06))
    clipped = scale * grad
    new_first = 0.9 * first_moment + 0.1 * clipped
    new_second = 0.999 * second_moment + 0.001 * clipped * clipped
    update = new_first / (1.0 - 0.9 ** 20) / (jnp.sqrt(new_second / (1.0 - 0.999 ** 20)) + 1e-08)
    new_master = master - 0.0001 * (update + 0.01 * master)
    new_weights = new_master.astype(jnp.bfloat16)
    return (dinputs.reshape(BATCH, FIN, C), update, new_master, new_first, new_second, new_weights)
```

```python
import jax
import jax.numpy as jnp
from jax import lax
from jax.sharding import Mesh
from jax.sharding import PartitionSpec as P


def norm_act(pre, gain, bias):
    center = pre - jnp.mean(pre, axis=-1, keepdims=True)
    spread = jnp.mean(center * center, axis=-1, keepdims=True)
    normed = center * lax.rsqrt(spread + 1e-05)
    return jax.nn.gelu(normed * gain + bias, approximate=False)


def local_pass(inputs, weights, ln_gain, ln_bias, projection, targets):
    clips, frames_in, chans = inputs.shape
    taps = weights.shape[0]
    frames_out = (frames_in - taps) // taps + 1
    windows = inputs[:, : frames_out * taps].reshape(clips, frames_out, taps, chans)
    kernel = weights.reshape(taps, chans, chans)
    pre = jnp.einsum("bfki,koi->bfo", windows, kernel, preferred_element_type=jnp.float32)
    act, pull = jax.vjp(lambda value: norm_act(value, ln_gain, ln_bias), pre)
    pooled = jnp.mean(act, axis=1).astype(jnp.bfloat16)
    predicted = jnp.dot(pooled, projection, preferred_element_type=jnp.float32)
    miss = (predicted - targets).astype(jnp.bfloat16)
    back = lax.dot_general(
        miss, projection, (((1,), (1,)), ((), ())), preferred_element_type=jnp.float32
    )
    upstream = jnp.broadcast_to(back[:, None, :] / frames_out, act.shape)
    dpre = pull(upstream)[0].astype(jnp.bfloat16)
    dwin = jnp.einsum("bfo,koi->bfki", dpre, kernel, preferred_element_type=jnp.float32).astype(
        jnp.bfloat16
    )
    dinput = dwin.reshape(clips, frames_out * taps, chans)
    tail = jnp.zeros((clips, frames_in - frames_out * taps, chans), jnp.bfloat16)
    return (windows, dpre, jnp.concatenate([dinput, tail], axis=1))


AXES = ("z", "x", "y", "core")
PLANE = ("x", "y", "core")


def exchange(value, axes):
    return lax.all_to_all(value, axes, 0, 0, tiled=False)


def spread(value, axes, count):
    return exchange(jnp.broadcast_to(value[None], (count,) + value.shape), axes)


def body(
    inputs, weights, ln_gain, ln_bias, projection, targets, master, first_moment, second_moment
):
    depth, plane = lax.axis_size("z"), lax.axis_size(PLANE)
    taps, width = weights.shape[0], ln_gain.shape[0]
    f32, bf16 = jnp.float32, jnp.bfloat16
    windows, dpre, input_grad = local_pass(inputs, weights, ln_gain, ln_bias, projection, targets)
    term = jnp.einsum("bfo,bfki->koi", dpre, windows, preferred_element_type=f32).astype(bf16)
    term = term.reshape(taps, depth, plane, width).transpose(2, 1, 0, 3)
    part = jnp.sum(exchange(term, PLANE).astype(f32), axis=0).astype(bf16)
    high = master.astype(bf16)
    low = (master - high.astype(f32)).astype(bf16)
    state = jnp.stack([high, low, first_moment.astype(bf16), second_moment.astype(bf16)])
    packed = jnp.concatenate([part, state], axis=0)
    column = spread(packed, "z", depth)
    grad = jnp.sum(column[:, :depth].astype(f32), axis=0)
    state = column[:, depth:].astype(f32)
    piece = jnp.full((8, 128), jnp.sum(grad * grad), f32)
    squares = jnp.sum(spread(piece, PLANE, plane)[:, 0, 0])
    scale = jnp.minimum(1.0, 1.0 / (jnp.sqrt(squares) + 1e-06))

    def advance(grad, master, first_moment, second_moment):
        clipped = scale * grad
        new_first = 0.9 * first_moment + 0.1 * clipped
        new_second = 0.999 * second_moment + 0.001 * clipped * clipped
        update = new_first / (1.0 - 0.9**20) / (jnp.sqrt(new_second / (1.0 - 0.999**20)) + 1e-08)
        new_master = master - 0.0001 * (update + 0.01 * master)
        return update, new_master, new_first, new_second

    mine = lax.dynamic_index_in_dim(grad, lax.axis_index("z"), 0, keepdims=False)
    update, new_master, new_first, new_second = advance(mine, master, first_moment, second_moment)
    rows = advance(grad, state[:, 0] + state[:, 1], state[:, 2], state[:, 3])[1].astype(bf16)
    whole = spread(rows, PLANE, plane)
    new_weights = whole.transpose(2, 1, 0, 3).reshape(taps, -1)
    return (input_grad, update, new_master, new_first, new_second, new_weights)


def solution(mesh):
    grid = Mesh(mesh.devices.reshape(16, 4, 4, 2), AXES)
    return jax.shard_map(
        body,
        mesh=grid,
        in_specs=(
            P(AXES, None, None),
            P(),
            P(),
            P(),
            P(),
            P(AXES, None),
            P(None, AXES),
            P(None, AXES),
            P(None, AXES),
        ),
        out_specs=(
            P(AXES, None, None),
            P(None, AXES),
            P(None, AXES),
            P(None, AXES),
            P(None, AXES),
            P(),
        ),
        check_vma=False,
    )
```

```python
import jax
import jax.numpy as jnp
from jax import lax
from jax.sharding import Mesh
from jax.sharding import PartitionSpec as P


def norm_act(pre, gain, bias):
    center = pre - jnp.mean(pre, axis=-1, keepdims=True)
    spread = jnp.mean(center * center, axis=-1, keepdims=True)
    normed = center * lax.rsqrt(spread + 1e-05)
    return jax.nn.gelu(normed * gain + bias, approximate=False)


def local_pass(inputs, weights, ln_gain, ln_bias, projection, targets):
    clips, frames_in, chans = inputs.shape
    taps = weights.shape[0]
    frames_out = (frames_in - taps) // taps + 1
    windows = inputs[:, : frames_out * taps].reshape(clips, frames_out, taps, chans)
    kernel = weights.reshape(taps, chans, chans)
    pre = jnp.einsum("bfki,koi->bfo", windows, kernel, preferred_element_type=jnp.float32)
    act, pull = jax.vjp(lambda value: norm_act(value, ln_gain, ln_bias), pre)
    pooled = jnp.mean(act, axis=1).astype(jnp.bfloat16)
    predicted = jnp.dot(pooled, projection, preferred_element_type=jnp.float32)
    miss = (predicted - targets).astype(jnp.bfloat16)
    back = lax.dot_general(
        miss, projection, (((1,), (1,)), ((), ())), preferred_element_type=jnp.float32
    )
    upstream = jnp.broadcast_to(back[:, None, :] / frames_out, act.shape)
    dpre = pull(upstream)[0].astype(jnp.bfloat16)
    dwin = jnp.einsum("bfo,koi->bfki", dpre, kernel, preferred_element_type=jnp.float32).astype(
        jnp.bfloat16
    )
    dinput = dwin.reshape(clips, frames_out * taps, chans)
    tail = jnp.zeros((clips, frames_in - frames_out * taps, chans), jnp.bfloat16)
    return (windows, dpre, jnp.concatenate([dinput, tail], axis=1))


AXES = ("z", "x", "y", "core")
PLANE = ("x", "y", "core")


def exchange(value, axes):
    return lax.all_to_all(value, axes, 0, 0, tiled=False)


def spread(value, axes, count):
    return exchange(jnp.broadcast_to(value[None], (count,) + value.shape), axes)


def body(
    inputs, weights, ln_gain, ln_bias, projection, targets, master, first_moment, second_moment
):
    depth, plane = lax.axis_size("z"), lax.axis_size(PLANE)
    taps, width = weights.shape[0], ln_gain.shape[0]
    f32, bf16 = jnp.float32, jnp.bfloat16
    windows, dpre, input_grad = local_pass(inputs, weights, ln_gain, ln_bias, projection, targets)
    term = jnp.einsum("bfo,bfki->koi", dpre, windows, preferred_element_type=f32).astype(bf16)
    term = term.reshape(taps, depth, plane, width).transpose(2, 1, 0, 3)
    part = jnp.sum(exchange(term, PLANE).astype(f32), axis=0).astype(bf16)
    high = master.astype(bf16)
    low = (master - high.astype(f32)).astype(bf16)
    state = jnp.stack([high, low, first_moment.astype(bf16), second_moment.astype(bf16)])
    packed = jnp.concatenate([part, state], axis=0)
    column = lax.all_gather(packed, "z")
    grad = jnp.sum(column[:, :depth].astype(f32), axis=0)
    state = column[:, depth:].astype(f32)
    piece = jnp.full((8, 128), jnp.sum(grad * grad), f32)
    squares = jnp.sum(spread(piece, PLANE, plane)[:, 0, 0])
    scale = jnp.minimum(1.0, 1.0 / (jnp.sqrt(squares) + 1e-06))

    def advance(grad, master, first_moment, second_moment):
        clipped = scale * grad
        new_first = 0.9 * first_moment + 0.1 * clipped
        new_second = 0.999 * second_moment + 0.001 * clipped * clipped
        update = new_first / (1.0 - 0.9**20) / (jnp.sqrt(new_second / (1.0 - 0.999**20)) + 1e-08)
        new_master = master - 0.0001 * (update + 0.01 * master)
        return update, new_master, new_first, new_second

    mine = lax.dynamic_index_in_dim(grad, lax.axis_index("z"), 0, keepdims=False)
    update, new_master, new_first, new_second = advance(mine, master, first_moment, second_moment)
    rows = advance(grad, state[:, 0] + state[:, 1], state[:, 2], state[:, 3])[1].astype(bf16)
    whole = spread(rows, PLANE, plane)
    new_weights = whole.transpose(2, 1, 0, 3).reshape(taps, -1)
    return (input_grad, update, new_master, new_first, new_second, new_weights)


def solution(mesh):
    grid = Mesh(mesh.devices.reshape(16, 4, 4, 2), AXES)
    return jax.shard_map(
        body,
        mesh=grid,
        in_specs=(
            P(AXES, None, None),
            P(),
            P(),
            P(),
            P(),
            P(AXES, None),
            P(None, AXES),
            P(None, AXES),
            P(None, AXES),
        ),
        out_specs=(
            P(AXES, None, None),
            P(None, AXES),
            P(None, AXES),
            P(None, AXES),
            P(None, AXES),
            P(),
        ),
        check_vma=False,
    )
```

```python
import jax
import jax.numpy as jnp
from jax import lax
from jax.experimental import pallas as pl
from jax.experimental.pallas import tpu as pltpu
from jax.sharding import Mesh
from jax.sharding import PartitionSpec as P


def norm_act(pre, gain, bias):
    center = pre - jnp.mean(pre, axis=-1, keepdims=True)
    spread = jnp.mean(center * center, axis=-1, keepdims=True)
    normed = center * lax.rsqrt(spread + 1e-05)
    return jax.nn.gelu(normed * gain + bias, approximate=False)


def local_pass(inputs, weights, ln_gain, ln_bias, projection, targets):
    clips, frames_in, chans = inputs.shape
    taps = weights.shape[0]
    frames_out = (frames_in - taps) // taps + 1
    windows = inputs[:, : frames_out * taps].reshape(clips, frames_out, taps, chans)
    kernel = weights.reshape(taps, chans, chans)
    pre = jnp.einsum("bfki,koi->bfo", windows, kernel, preferred_element_type=jnp.float32)
    act, pull = jax.vjp(lambda value: norm_act(value, ln_gain, ln_bias), pre)
    pooled = jnp.mean(act, axis=1).astype(jnp.bfloat16)
    predicted = jnp.dot(pooled, projection, preferred_element_type=jnp.float32)
    miss = (predicted - targets).astype(jnp.bfloat16)
    back = lax.dot_general(
        miss, projection, (((1,), (1,)), ((), ())), preferred_element_type=jnp.float32
    )
    upstream = jnp.broadcast_to(back[:, None, :] / frames_out, act.shape)
    dpre = pull(upstream)[0].astype(jnp.bfloat16)
    dwin = jnp.einsum("bfo,koi->bfki", dpre, kernel, preferred_element_type=jnp.float32).astype(
        jnp.bfloat16
    )
    dinput = dwin.reshape(clips, frames_out * taps, chans)
    tail = jnp.zeros((clips, frames_in - frames_out * taps, chans), jnp.bfloat16)
    return (windows, dpre, jnp.concatenate([dinput, tail], axis=1))


AXES = ("z", "x", "y", "core")
PLANE = ("x", "y", "core")
LANES = 128


def plane_sum(recv, master, first, second, out, rows):
    taps, width = master.shape
    depth = recv.shape[1]
    total = recv[0].astype(jnp.float32)
    for src in range(1, recv.shape[0]):
        total += recv[src].astype(jnp.float32)
    out[0:depth, :] = total.astype(jnp.bfloat16)
    rows[...] = jnp.zeros_like(rows)
    high = master[...].astype(jnp.bfloat16).astype(jnp.float32)
    for row, value in enumerate((high, master[...] - high, first[...], second[...])):
        for tap in range(taps):
            rows[row : row + 1, tap * width : (tap + 1) * width] = value[tap : tap + 1, :]
    out[depth:, :] = rows[...].astype(jnp.bfloat16)


def column_sum(column, grad, piece):
    depth = column.shape[0]
    total = column[0, 0:depth, :].astype(jnp.float32)
    for src in range(1, depth):
        total += column[src, 0:depth, :].astype(jnp.float32)
    grad[...] = total
    squares = jnp.sum(jnp.sum(total * total, axis=0, keepdims=True), axis=1, keepdims=True)
    piece[...] = jnp.broadcast_to(squares[None], piece.shape)


def advance(scale, grad, master, first_moment, second_moment):
    clipped = scale * grad
    new_first = 0.9 * first_moment + 0.1 * clipped
    new_second = 0.999 * second_moment + 0.001 * clipped * clipped
    update = new_first / (1.0 - 0.9**20) / (jnp.sqrt(new_second / (1.0 - 0.999**20)) + 1e-08)
    new_master = master - 0.0001 * (update + 0.01 * master)
    return update, new_master, new_first, new_second


def plane_update(pieces, grad, column, out, scale_out, state, rows, block, sems):
    depth, taps = grad.shape[0], 2
    squares = jnp.sum(pieces[...], axis=0)[0:1, 0:1]
    scale = jnp.minimum(1.0, 1.0 / (jnp.sqrt(squares) + 1e-06))
    scale_out[...] = jnp.broadcast_to(scale, scale_out.shape)
    state[...] = column[:, depth:, :].astype(jnp.float32)
    master = state[:, 0, :] + state[:, 1, :]
    new_master = advance(scale, grad[...], master, state[:, 2, :], state[:, 3, :])[1]
    parts = grad.shape[1] // LANES // taps
    for tap in range(taps):
        for part in range(parts):
            start = (tap * parts + part) * LANES
            rows[:, part * taps + tap, :] = new_master[:, start : start + LANES]
    block[...] = rows[...].astype(jnp.bfloat16)
    copies = [
        pltpu.make_async_copy(block, out.at[peer], sems.at[peer]) for peer in range(out.shape[0])
    ]
    for copy in copies:
        copy.start()
    for copy in copies:
        copy.wait()


VMEM = pl.BlockSpec(memory_space=pltpu.VMEM)
ANY = pl.BlockSpec(memory_space=pl.ANY)


def exchange(value, axes):
    return lax.all_to_all(value, axes, 0, 0, tiled=False)


def body(
    inputs, weights, ln_gain, ln_bias, projection, targets, master, first_moment, second_moment
):
    depth, plane = lax.axis_size("z"), lax.axis_size(PLANE)
    taps, width = weights.shape[0], ln_gain.shape[0]
    f32, bf16 = jnp.float32, jnp.bfloat16
    shape = jax.ShapeDtypeStruct
    row = taps * width
    windows, dpre, input_grad = local_pass(inputs, weights, ln_gain, ln_bias, projection, targets)
    term = jnp.einsum("bfo,bfki->oki", dpre, windows, preferred_element_type=f32).astype(bf16)
    term = term.reshape(depth, plane, row).transpose(1, 0, 2)
    packed = pl.pallas_call(
        plane_sum,
        out_shape=shape((depth + 8, row), bf16),
        in_specs=[VMEM] * 4,
        out_specs=VMEM,
        scratch_shapes=[pltpu.VMEM((8, row), f32)],
        name="plane_sum",
    )(exchange(term, PLANE), master, first_moment, second_moment)
    column = lax.all_gather(packed, "z")
    grad, piece = pl.pallas_call(
        column_sum,
        out_shape=(shape((depth, row), f32), shape((plane, 8, LANES), f32)),
        in_specs=[VMEM],
        out_specs=(VMEM, VMEM),
        name="column_sum",
    )(column)
    rows, scale = pl.pallas_call(
        plane_update,
        out_shape=(shape((plane, depth, row // LANES, LANES), bf16), shape((8, LANES), f32)),
        in_specs=[VMEM] * 3,
        out_specs=(ANY, VMEM),
        scratch_shapes=[
            pltpu.VMEM((depth, 8, row), f32),
            pltpu.VMEM((depth, row // LANES, LANES), f32),
            pltpu.VMEM((depth, row // LANES, LANES), bf16),
            pltpu.SemaphoreType.DMA((plane,)),
        ],
        name="plane_update",
    )(exchange(piece, PLANE), grad, column)
    mine = lax.dynamic_slice_in_dim(grad, lax.axis_index("z"), 1, 0).reshape(taps, width)
    update, new_master, new_first, new_second = advance(
        scale[0, 0], mine, master, first_moment, second_moment
    )
    whole = exchange(rows, PLANE).transpose(1, 0, 2, 3)
    whole = whole.reshape(depth * plane * width // LANES, taps, LANES).transpose(1, 0, 2)
    new_weights = whole.reshape(taps, -1)
    return (input_grad, update, new_master, new_first, new_second, new_weights)


def solution(mesh):
    grid = Mesh(mesh.devices.reshape(16, 4, 4, 2), AXES)
    return jax.shard_map(
        body,
        mesh=grid,
        in_specs=(
            P(AXES, None, None),
            P(),
            P(),
            P(),
            P(),
            P(AXES, None),
            P(None, AXES),
            P(None, AXES),
            P(None, AXES),
        ),
        out_specs=(
            P(AXES, None, None),
            P(None, AXES),
            P(None, AXES),
            P(None, AXES),
            P(None, AXES),
            P(),
        ),
        check_vma=False,
    )
```

```python
import jax
import jax.numpy as jnp
from jax import lax
from jax.experimental import pallas as pl
from jax.experimental.pallas import tpu as pltpu
from jax.sharding import Mesh
from jax.sharding import PartitionSpec as P


def norm_act(pre, gain, bias):
    center = pre - jnp.mean(pre, axis=-1, keepdims=True)
    spread = jnp.mean(center * center, axis=-1, keepdims=True)
    normed = center * lax.rsqrt(spread + 1e-05)
    return jax.nn.gelu(normed * gain + bias, approximate=False)


def local_pass(inputs, weights, ln_gain, ln_bias, projection, targets):
    clips, frames_in, chans = inputs.shape
    taps = weights.shape[0]
    frames_out = (frames_in - taps) // taps + 1
    windows = inputs[:, : frames_out * taps].reshape(clips, frames_out, taps, chans)
    kernel = weights.reshape(taps, chans, chans)
    pre = jnp.einsum("bfki,koi->bfo", windows, kernel, preferred_element_type=jnp.float32)
    act, pull = jax.vjp(lambda value: norm_act(value, ln_gain, ln_bias), pre)
    pooled = jnp.mean(act, axis=1).astype(jnp.bfloat16)
    predicted = jnp.dot(pooled, projection, preferred_element_type=jnp.float32)
    miss = (predicted - targets).astype(jnp.bfloat16)
    back = lax.dot_general(
        miss, projection, (((1,), (1,)), ((), ())), preferred_element_type=jnp.float32
    )
    upstream = jnp.broadcast_to(back[:, None, :] / frames_out, act.shape)
    dpre = pull(upstream)[0].astype(jnp.bfloat16)
    dwin = jnp.einsum("bfo,koi->bfki", dpre, kernel, preferred_element_type=jnp.float32).astype(
        jnp.bfloat16
    )
    dinput = dwin.reshape(clips, frames_out * taps, chans)
    tail = jnp.zeros((clips, frames_in - frames_out * taps, chans), jnp.bfloat16)
    return (windows, dpre, jnp.concatenate([dinput, tail], axis=1))


AXES = ("z", "x", "y", "core")
PLANE = ("x", "y", "core")
LANES = 128
LIMIT = 4 * 2**20


def plane_sum(recv, out):
    peers, taps, depth, width = recv.shape
    parts = width // LANES
    for tap in range(taps):
        total = recv[0, tap].astype(jnp.float32)
        for src in range(1, peers):
            total += recv[src, tap].astype(jnp.float32)
        for part in range(parts):
            out[:, part * taps + tap, :] = total[:, part * LANES : (part + 1) * LANES]


def column_pack(recv, master, first, second, grad, out):
    total = jnp.sum(recv[...], axis=0)
    grad[...] = total
    high = master[...].astype(jnp.bfloat16)
    low = (master[...] - high.astype(jnp.float32)).astype(jnp.bfloat16)
    rows = (total.astype(jnp.bfloat16), high, low)
    rows += (first[...].astype(jnp.bfloat16), second[...].astype(jnp.bfloat16))
    for index, row in enumerate(rows):
        for peer in range(out.shape[0]):
            out[peer, index] = row


def column_squares(column, piece):
    grad = column[:, 0].astype(jnp.float32)
    squares = jnp.sum(grad * grad, axis=0)
    squares = jnp.sum(jnp.sum(squares, axis=0, keepdims=True), axis=1, keepdims=True)
    piece[...] = jnp.broadcast_to(squares[None], piece.shape)


def advance(scale, grad, master, first_moment, second_moment):
    clipped = scale * grad
    new_first = 0.9 * first_moment + 0.1 * clipped
    new_second = 0.999 * second_moment + 0.001 * clipped * clipped
    update = new_first / (1.0 - 0.9**20) / (jnp.sqrt(new_second / (1.0 - 0.999**20)) + 1e-08)
    new_master = master - 0.0001 * (update + 0.01 * master)
    return update, new_master, new_first, new_second


def plane_update(pieces, column, out, scale_out, block, sems):
    squares = jnp.sum(pieces[...], axis=0)[0:1, 0:1]
    scale = jnp.minimum(1.0, 1.0 / (jnp.sqrt(squares) + 1e-06))
    scale_out[...] = jnp.broadcast_to(scale, scale_out.shape)
    grad, high, low, first, second = (column[:, i].astype(jnp.float32) for i in range(5))
    block[...] = advance(scale[None], grad, high + low, first, second)[1].astype(jnp.bfloat16)
    copies = [
        pltpu.make_async_copy(block, out.at[peer], sems.at[peer]) for peer in range(out.shape[0])
    ]
    for copy in copies:
        copy.start()
    for copy in copies:
        copy.wait()


VMEM = pl.BlockSpec(memory_space=pltpu.VMEM)
ANY = pl.BlockSpec(memory_space=pl.ANY)


def local(kernel, out_shape, count, out_specs=VMEM, scratch=()):
    return pl.pallas_call(
        kernel,
        out_shape=out_shape,
        in_specs=[VMEM] * count,
        out_specs=out_specs,
        scratch_shapes=list(scratch),
        compiler_params=pltpu.CompilerParams(vmem_limit_bytes=LIMIT),
        name=kernel.__name__,
    )


def exchange(value, axes):
    return lax.all_to_all(value, axes, 0, 0, tiled=False)


def to_rows(shard):
    taps = shard.shape[0]
    return shard.reshape(taps, -1, LANES).transpose(1, 0, 2).reshape(-1, LANES)


def from_rows(rows, taps):
    return rows.reshape(-1, taps, LANES).transpose(1, 0, 2).reshape(taps, -1)


def body(
    inputs, weights, ln_gain, ln_bias, projection, targets, master, first_moment, second_moment
):
    depth, plane = lax.axis_size("z"), lax.axis_size(PLANE)
    taps, width = weights.shape[0], ln_gain.shape[0]
    tile = (taps * width // LANES, LANES)
    f32, bf16 = jnp.float32, jnp.bfloat16
    shape = jax.ShapeDtypeStruct
    windows, dpre, input_grad = local_pass(inputs, weights, ln_gain, ln_bias, projection, targets)
    order = jnp.arange(width).reshape(depth, plane).T.reshape(-1)
    pick = (jnp.arange(width)[:, None] == order[None, :]).astype(bf16)
    moved = jnp.einsum("bfo,op->bfp", dpre, pick, preferred_element_type=f32).astype(bf16)
    term = jnp.einsum("bfo,bfki->koi", moved, windows, preferred_element_type=f32).astype(bf16)
    term = term.reshape(taps, plane, depth, width).transpose(1, 0, 2, 3)
    part = local(plane_sum, shape((depth,) + tile, f32), 1)(exchange(term, PLANE))
    shards = [to_rows(value) for value in (master, first_moment, second_moment)]
    grad, packed = local(
        column_pack, (shape(tile, f32), shape((depth, 5) + tile, bf16)), 4, (VMEM, VMEM)
    )(exchange(part, "z"), *shards)
    column = exchange(packed, "z")
    piece = local(column_squares, shape((plane, 8, LANES), f32), 1)(column)
    rows, scale = local(
        plane_update,
        (shape((plane, depth) + tile, bf16), shape((8, LANES), f32)),
        2,
        (ANY, VMEM),
        (pltpu.VMEM((depth,) + tile, bf16), pltpu.SemaphoreType.DMA((plane,))),
    )(exchange(piece, PLANE), column)
    fresh = [from_rows(value, taps) for value in advance(scale, grad, *shards)]
    update, new_master, new_first, new_second = fresh
    whole = exchange(rows, PLANE).transpose(1, 0, 2, 3)
    new_weights = from_rows(whole, taps)
    return (input_grad, update, new_master, new_first, new_second, new_weights)


def solution(mesh):
    grid = Mesh(mesh.devices.reshape(16, 4, 4, 2), AXES)
    return jax.shard_map(
        body,
        mesh=grid,
        in_specs=(
            P(AXES, None, None),
            P(),
            P(),
            P(),
            P(),
            P(AXES, None),
            P(None, AXES),
            P(None, AXES),
            P(None, AXES),
        ),
        out_specs=(
            P(AXES, None, None),
            P(None, AXES),
            P(None, AXES),
            P(None, AXES),
            P(None, AXES),
            P(),
        ),
        check_vma=False,
    )
```

```python
import jax
import jax.numpy as jnp
from jax import lax
from jax.experimental import pallas as pl
from jax.experimental.pallas import tpu as pltpu
from jax.sharding import Mesh
from jax.sharding import PartitionSpec as P


def norm_act(pre, gain, bias):
    center = pre - jnp.mean(pre, axis=-1, keepdims=True)
    spread = jnp.mean(center * center, axis=-1, keepdims=True)
    normed = center * lax.rsqrt(spread + 1e-05)
    return jax.nn.gelu(normed * gain + bias, approximate=False)


def local_pass(inputs, weights, ln_gain, ln_bias, projection, targets):
    clips, frames_in, chans = inputs.shape
    taps = weights.shape[0]
    frames_out = (frames_in - taps) // taps + 1
    windows = inputs[:, : frames_out * taps].reshape(clips, frames_out, taps, chans)
    kernel = weights.reshape(taps, chans, chans)
    pre = jnp.einsum("bfki,koi->bfo", windows, kernel, preferred_element_type=jnp.float32)
    act, pull = jax.vjp(lambda value: norm_act(value, ln_gain, ln_bias), pre)
    pooled = jnp.mean(act, axis=1).astype(jnp.bfloat16)
    predicted = jnp.dot(pooled, projection, preferred_element_type=jnp.float32)
    miss = (predicted - targets).astype(jnp.bfloat16)
    back = lax.dot_general(
        miss, projection, (((1,), (1,)), ((), ())), preferred_element_type=jnp.float32
    )
    upstream = jnp.broadcast_to(back[:, None, :] / frames_out, act.shape)
    dpre = pull(upstream)[0].astype(jnp.bfloat16)
    dwin = jnp.einsum("bfo,koi->bfki", dpre, kernel, preferred_element_type=jnp.float32).astype(
        jnp.bfloat16
    )
    dinput = dwin.reshape(clips, frames_out * taps, chans)
    tail = jnp.zeros((clips, frames_in - frames_out * taps, chans), jnp.bfloat16)
    return (windows, dpre, jnp.concatenate([dinput, tail], axis=1))


AXES = ("z", "x", "y", "core")
PLANE = ("x", "y", "core")
LANES = 128
LIMIT = 4 * 2**20


def plane_sum(recv, master, first, second, out, rows):
    peers, taps, depth, width = recv.shape
    parts = width // LANES
    for tap in range(taps):
        total = recv[0, tap].astype(jnp.float32)
        for src in range(1, peers):
            total += recv[src, tap].astype(jnp.float32)
        for part in range(parts):
            rows[:, part * taps + tap, :] = total[:, part * LANES : (part + 1) * LANES]
    out[0:depth] = rows[...].astype(jnp.bfloat16)
    high = master[...].astype(jnp.bfloat16)
    out[depth] = high
    out[depth + 1] = (master[...] - high.astype(jnp.float32)).astype(jnp.bfloat16)
    out[depth + 2] = first[...].astype(jnp.bfloat16)
    out[depth + 3] = second[...].astype(jnp.bfloat16)


def column_sum(column, grad, piece):
    depth = column.shape[0]
    total = column[0, 0:depth].astype(jnp.float32)
    for src in range(1, depth):
        total += column[src, 0:depth].astype(jnp.float32)
    grad[...] = total
    squares = jnp.sum(total * total, axis=0)
    squares = jnp.sum(jnp.sum(squares, axis=0, keepdims=True), axis=1, keepdims=True)
    piece[...] = jnp.broadcast_to(squares[None], piece.shape)


def advance(scale, grad, master, first_moment, second_moment):
    clipped = scale * grad
    new_first = 0.9 * first_moment + 0.1 * clipped
    new_second = 0.999 * second_moment + 0.001 * clipped * clipped
    update = new_first / (1.0 - 0.9**20) / (jnp.sqrt(new_second / (1.0 - 0.999**20)) + 1e-08)
    new_master = master - 0.0001 * (update + 0.01 * master)
    return update, new_master, new_first, new_second


def plane_update(pieces, grad, column, out, scale_out, block, sems):
    depth = column.shape[0]
    squares = jnp.sum(pieces[...], axis=0)[0:1, 0:1]
    scale = jnp.minimum(1.0, 1.0 / (jnp.sqrt(squares) + 1e-06))
    scale_out[...] = jnp.broadcast_to(scale, scale_out.shape)
    high, low, first, second = (column[:, depth + i].astype(jnp.float32) for i in range(4))
    new_master = advance(scale[None], grad[...], high + low, first, second)[1]
    block[...] = new_master.astype(jnp.bfloat16)
    copies = [
        pltpu.make_async_copy(block, out.at[peer], sems.at[peer]) for peer in range(out.shape[0])
    ]
    for copy in copies:
        copy.start()
    for copy in copies:
        copy.wait()


VMEM = pl.BlockSpec(memory_space=pltpu.VMEM)
ANY = pl.BlockSpec(memory_space=pl.ANY)


def local(kernel, out_shape, count, out_specs=VMEM, scratch=()):
    return pl.pallas_call(
        kernel,
        out_shape=out_shape,
        in_specs=[VMEM] * count,
        out_specs=out_specs,
        scratch_shapes=list(scratch),
        compiler_params=pltpu.CompilerParams(vmem_limit_bytes=LIMIT),
        name=kernel.__name__,
    )


def exchange(value, axes):
    return lax.all_to_all(value, axes, 0, 0, tiled=False)


def to_rows(shard):
    taps = shard.shape[0]
    return shard.reshape(taps, -1, LANES).transpose(1, 0, 2).reshape(-1, LANES)


def from_rows(rows, taps):
    return rows.reshape(-1, taps, LANES).transpose(1, 0, 2).reshape(taps, -1)


def body(
    inputs, weights, ln_gain, ln_bias, projection, targets, master, first_moment, second_moment
):
    depth, plane = lax.axis_size("z"), lax.axis_size(PLANE)
    taps, width = weights.shape[0], ln_gain.shape[0]
    tile = (taps * width // LANES, LANES)
    f32, bf16 = jnp.float32, jnp.bfloat16
    shape = jax.ShapeDtypeStruct
    windows, dpre, input_grad = local_pass(inputs, weights, ln_gain, ln_bias, projection, targets)
    term = jnp.einsum("bfo,bfki->koi", dpre, windows, preferred_element_type=f32).astype(bf16)
    term = term.reshape(taps, depth, plane, width).transpose(2, 0, 1, 3)
    shards = [to_rows(value) for value in (master, first_moment, second_moment)]
    packed = local(
        plane_sum, shape((depth + 4,) + tile, bf16), 4, VMEM, (pltpu.VMEM((depth,) + tile, f32),)
    )(exchange(term, PLANE), *shards)
    column = lax.all_gather(packed, "z")
    grad, piece = local(
        column_sum,
        (shape((depth,) + tile, f32), shape((plane, 8, LANES), f32)),
        1,
        (VMEM, VMEM),
    )(column)
    rows, scale = local(
        plane_update,
        (shape((plane, depth) + tile, bf16), shape((8, LANES), f32)),
        3,
        (ANY, VMEM),
        (pltpu.VMEM((depth,) + tile, bf16), pltpu.SemaphoreType.DMA((plane,))),
    )(exchange(piece, PLANE), grad, column)
    grad = lax.dynamic_index_in_dim(grad, lax.axis_index("z"), 0, keepdims=False)
    fresh = [from_rows(value, taps) for value in advance(scale, grad, *shards)]
    update, new_master, new_first, new_second = fresh
    whole = exchange(rows, PLANE).transpose(1, 0, 2, 3)
    new_weights = from_rows(whole, taps)
    return (input_grad, update, new_master, new_first, new_second, new_weights)


def solution(mesh):
    grid = Mesh(mesh.devices.reshape(16, 4, 4, 2), AXES)
    return jax.shard_map(
        body,
        mesh=grid,
        in_specs=(
            P(AXES, None, None),
            P(),
            P(),
            P(),
            P(),
            P(AXES, None),
            P(None, AXES),
            P(None, AXES),
            P(None, AXES),
        ),
        out_specs=(
            P(AXES, None, None),
            P(None, AXES),
            P(None, AXES),
            P(None, AXES),
            P(None, AXES),
            P(),
        ),
        check_vma=False,
    )
```

```python
import jax
import jax.numpy as jnp
from jax import lax
from jax.experimental import pallas as pl
from jax.experimental.pallas import tpu as pltpu
from jax.sharding import Mesh
from jax.sharding import PartitionSpec as P


def norm_act(pre, gain, bias):
    center = pre - jnp.mean(pre, axis=-1, keepdims=True)
    spread = jnp.mean(center * center, axis=-1, keepdims=True)
    normed = center * lax.rsqrt(spread + 1e-05)
    return jax.nn.gelu(normed * gain + bias, approximate=False)


def local_pass(inputs, weights, ln_gain, ln_bias, projection, targets):
    clips, frames_in, chans = inputs.shape
    taps = weights.shape[0]
    frames_out = (frames_in - taps) // taps + 1
    windows = inputs[:, : frames_out * taps].reshape(clips, frames_out, taps, chans)
    kernel = weights.reshape(taps, chans, chans)
    pre = jnp.einsum("bfki,koi->bfo", windows, kernel, preferred_element_type=jnp.float32)
    act, pull = jax.vjp(lambda value: norm_act(value, ln_gain, ln_bias), pre)
    pooled = jnp.mean(act, axis=1).astype(jnp.bfloat16)
    predicted = jnp.dot(pooled, projection, preferred_element_type=jnp.float32)
    miss = (predicted - targets).astype(jnp.bfloat16)
    back = lax.dot_general(
        miss, projection, (((1,), (1,)), ((), ())), preferred_element_type=jnp.float32
    )
    upstream = jnp.broadcast_to(back[:, None, :] / frames_out, act.shape)
    dpre = pull(upstream)[0].astype(jnp.bfloat16)
    dwin = jnp.einsum("bfo,koi->bfki", dpre, kernel, preferred_element_type=jnp.float32).astype(
        jnp.bfloat16
    )
    dinput = dwin.reshape(clips, frames_out * taps, chans)
    tail = jnp.zeros((clips, frames_in - frames_out * taps, chans), jnp.bfloat16)
    return (windows, dpre, jnp.concatenate([dinput, tail], axis=1))


AXES = ("z", "x", "y", "core")
PLANE = ("x", "y", "core")
LANES = 128
LIMIT = 4 * 2**20


def plane_sum(recv, master, first, second, out, rows):
    peers, taps, depth, width = recv.shape
    parts = width // LANES
    for tap in range(taps):
        total = recv[0, tap].astype(jnp.float32)
        for src in range(1, peers):
            total += recv[src, tap].astype(jnp.float32)
        for part in range(parts):
            rows[:, part * taps + tap, :] = total[:, part * LANES : (part + 1) * LANES]
    out[0:depth] = rows[...].astype(jnp.bfloat16)
    high = master[...].astype(jnp.bfloat16)
    out[depth] = high
    out[depth + 1] = (master[...] - high.astype(jnp.float32)).astype(jnp.bfloat16)
    out[depth + 2] = first[...].astype(jnp.bfloat16)
    out[depth + 3] = second[...].astype(jnp.bfloat16)


def column_sum(column, grad, piece):
    depth = column.shape[0]
    total = column[0, 0:depth].astype(jnp.float32)
    for src in range(1, depth):
        total += column[src, 0:depth].astype(jnp.float32)
    grad[...] = total
    squares = jnp.sum(total * total, axis=0)
    squares = jnp.sum(jnp.sum(squares, axis=0, keepdims=True), axis=1, keepdims=True)
    piece[...] = jnp.broadcast_to(squares[None], piece.shape)


def advance(scale, grad, master, first_moment, second_moment):
    clipped = scale * grad
    new_first = 0.9 * first_moment + 0.1 * clipped
    new_second = 0.999 * second_moment + 0.001 * clipped * clipped
    update = new_first / (1.0 - 0.9**20) / (jnp.sqrt(new_second / (1.0 - 0.999**20)) + 1e-08)
    new_master = master - 0.0001 * (update + 0.01 * master)
    return update, new_master, new_first, new_second


def plane_update(pieces, grad, column, out, scale_out):
    depth = column.shape[0]
    squares = jnp.sum(pieces[...], axis=0)[0:1, 0:1]
    scale = jnp.minimum(1.0, 1.0 / (jnp.sqrt(squares) + 1e-06))
    scale_out[...] = jnp.broadcast_to(scale, scale_out.shape)
    high, low, first, second = (column[:, depth + i].astype(jnp.float32) for i in range(4))
    new_master = advance(scale[None], grad[...], high + low, first, second)[1]
    block = new_master.astype(jnp.bfloat16)
    for peer in range(out.shape[0]):
        out[peer] = block


def place(core, source, *refs):
    out, sems = refs[-2:]
    copies = [
        pltpu.make_async_copy(source.at[:, z], out.at[z, :, core[0]], sems.at[z])
        for z in range(out.shape[0])
    ]
    for copy in copies:
        copy.start()
    for copy in copies:
        copy.wait()


VMEM = pl.BlockSpec(memory_space=pltpu.VMEM)
SMEM = pl.BlockSpec(memory_space=pltpu.SMEM)
ANY = pl.BlockSpec(memory_space=pl.ANY)


def local(kernel, out_shape, count, out_specs=VMEM, scratch=()):
    return pl.pallas_call(
        kernel,
        out_shape=out_shape,
        in_specs=[VMEM] * count,
        out_specs=out_specs,
        scratch_shapes=list(scratch),
        compiler_params=pltpu.CompilerParams(vmem_limit_bytes=LIMIT),
        name=kernel.__name__,
    )


def put_half(core, half, whole=None):
    peers, depth, *tile = half.shape
    size = half.size * half.dtype.itemsize
    return pl.pallas_call(
        place,
        out_shape=jax.ShapeDtypeStruct((depth, peers, 2, *tile), half.dtype),
        in_specs=[SMEM, VMEM] + [ANY] * (whole is not None),
        out_specs=ANY,
        scratch_shapes=[pltpu.SemaphoreType.DMA((depth,))],
        input_output_aliases={2: 0} if whole is not None else {},
        compiler_params=pltpu.CompilerParams(vmem_limit_bytes=LIMIT),
        cost_estimate=pl.CostEstimate(flops=0, transcendentals=0, bytes_accessed=2 * size),
        name="put_half",
    )(core, half, *(() if whole is None else (whole,)))


def exchange(value, axes):
    return lax.all_to_all(value, axes, 0, 0, tiled=False)


def to_rows(shard):
    taps = shard.shape[0]
    return shard.reshape(taps, -1, LANES).transpose(1, 0, 2).reshape(-1, LANES)


def from_rows(rows, taps):
    return rows.reshape(-1, taps, LANES).transpose(1, 0, 2).reshape(taps, -1)


def body(
    inputs, weights, ln_gain, ln_bias, projection, targets, master, first_moment, second_moment
):
    depth, plane = lax.axis_size("z"), lax.axis_size(PLANE)
    taps, width = weights.shape[0], ln_gain.shape[0]
    tile = (taps * width // LANES, LANES)
    f32, bf16 = jnp.float32, jnp.bfloat16
    shape = jax.ShapeDtypeStruct
    windows, dpre, input_grad = local_pass(inputs, weights, ln_gain, ln_bias, projection, targets)
    term = jnp.einsum("bfo,bfki->koi", dpre, windows, preferred_element_type=f32).astype(bf16)
    term = term.reshape(taps, depth, plane, width).transpose(2, 0, 1, 3)
    recv, input_grad = lax.optimization_barrier((exchange(term, PLANE), input_grad))
    shards = [to_rows(value) for value in (master, first_moment, second_moment)]
    packed = local(
        plane_sum, shape((depth + 4,) + tile, bf16), 4, VMEM, (pltpu.VMEM((depth,) + tile, f32),)
    )(recv, *shards)
    column = lax.all_gather(packed, "z")
    grad, piece = local(
        column_sum,
        (shape((depth,) + tile, f32), shape((plane, 8, LANES), f32)),
        1,
        (VMEM, VMEM),
    )(column)
    rows, scale = local(
        plane_update,
        (shape((plane // 2, depth) + tile, bf16), shape((8, LANES), f32)),
        3,
        (VMEM, VMEM),
    )(exchange(piece, PLANE), grad, column)
    grad = lax.dynamic_index_in_dim(grad, lax.axis_index("z"), 0, keepdims=False)
    fresh = [from_rows(value, taps) for value in advance(scale, grad, *shards)]
    update, new_master, new_first, new_second = fresh
    own = exchange(rows, PLANE[:2])
    other = lax.ppermute(own, "core", [(0, 1), (1, 0)])
    core = lax.axis_index("core").reshape(1)
    whole = put_half(core, own)
    whole = put_half(1 - core, other, whole)
    new_weights = from_rows(whole, taps)
    return (input_grad, update, new_master, new_first, new_second, new_weights)


def solution(mesh):
    grid = Mesh(mesh.devices.reshape(16, 4, 4, 2), AXES)
    return jax.shard_map(
        body,
        mesh=grid,
        in_specs=(
            P(AXES, None, None),
            P(),
            P(),
            P(),
            P(),
            P(AXES, None),
            P(None, AXES),
            P(None, AXES),
            P(None, AXES),
        ),
        out_specs=(
            P(AXES, None, None),
            P(None, AXES),
            P(None, AXES),
            P(None, AXES),
            P(None, AXES),
            P(),
        ),
        check_vma=False,
    )
```

```python
import math

import jax
import jax.numpy as jnp
from jax import lax
from jax.experimental import pallas as pl
from jax.experimental.pallas import tpu as pltpu
from jax.sharding import Mesh
from jax.sharding import PartitionSpec as P


AXES = ("z", "x", "y", "core")
PLANE = ("x", "y", "core")
LANES = 128
LIMIT = 4 * 2**20
VMEM = pl.BlockSpec(memory_space=pltpu.VMEM)


def chunks(frames):
    return [slice(start, min(start + 8, frames)) for start in range(0, frames, 8)]


def middle(pre, gain, bias, projection, targets, dpre, normed, slope, deviation):
    clips, frames, width = pre.shape
    gains, biases = gain[...][None], bias[...][None]
    pooled = jnp.zeros((clips, width), jnp.float32)
    for rows in chunks(frames):
        value = pre[:, rows, :]
        center = value - jnp.mean(value, axis=-1, keepdims=True)
        spread = jnp.mean(center * center, axis=-1, keepdims=True)
        inverse = lax.rsqrt(spread + 1e-05)
        normal = center * inverse
        point = normal * gains + biases
        share = 0.5 + 0.5 * lax.erf(point * math.sqrt(0.5))
        bell = jnp.exp(-0.5 * point * point) * (1.0 / math.sqrt(2.0 * math.pi))
        pooled += jnp.sum(point * share, axis=1)
        normed[:, rows, :] = normal
        slope[:, rows, :] = (share + point * bell) * gains
        deviation[:, rows, :] = jnp.broadcast_to(inverse, inverse.shape[:2] + (LANES,))
    pooled = (pooled / frames).astype(jnp.bfloat16)
    predicted = jnp.dot(pooled, projection[...], preferred_element_type=jnp.float32)
    miss = (predicted - targets[...]).astype(jnp.bfloat16)
    back = lax.dot_general(
        miss, projection[...], (((1,), (1,)), ((), ())), preferred_element_type=jnp.float32
    )
    upstream = (back / frames)[:, None, :]
    for rows in chunks(frames):
        normal = normed[:, rows, :]
        grad = slope[:, rows, :] * upstream
        first = jnp.mean(grad, axis=-1, keepdims=True)
        second = jnp.mean(grad * normal, axis=-1, keepdims=True)
        inverse = deviation[:, rows, 0:1]
        dpre[:, rows, :] = (inverse * (grad - first - normal * second)).astype(jnp.bfloat16)


def local_pass(inputs, weights, ln_gain, ln_bias, projection, targets):
    clips, frames_in, chans = inputs.shape
    taps = weights.shape[0]
    frames_out = (frames_in - taps) // taps + 1
    windows = inputs[:, : frames_out * taps].reshape(clips, frames_out, taps, chans)
    kernel = weights.reshape(taps, chans, chans)
    pre = jnp.einsum("bfki,koi->bfo", windows, kernel, preferred_element_type=jnp.float32)
    dpre = local(
        middle,
        jax.ShapeDtypeStruct(pre.shape, jnp.bfloat16),
        5,
        VMEM,
        (
            pltpu.VMEM(pre.shape, jnp.float32),
            pltpu.VMEM(pre.shape, jnp.float32),
            pltpu.VMEM(pre.shape[:2] + (LANES,), jnp.float32),
        ),
    )(pre, ln_gain[None], ln_bias[None], projection, targets)
    dwin = jnp.einsum("bfo,koi->bfki", dpre, kernel, preferred_element_type=jnp.float32).astype(
        jnp.bfloat16
    )
    dinput = dwin.reshape(clips, frames_out * taps, chans)
    tail = jnp.zeros((clips, frames_in - frames_out * taps, chans), jnp.bfloat16)
    return (windows, dpre, jnp.concatenate([dinput, tail], axis=1))


def plane_sum(recv, master, first, second, out, rows):
    peers, taps, depth, width = recv.shape
    parts = width // LANES
    for tap in range(taps):
        total = recv[0, tap].astype(jnp.float32)
        for src in range(1, peers):
            total += recv[src, tap].astype(jnp.float32)
        for part in range(parts):
            rows[:, part * taps + tap, :] = total[:, part * LANES : (part + 1) * LANES]
    out[0:depth] = rows[...].astype(jnp.bfloat16)
    high = master[...].astype(jnp.bfloat16)
    out[depth] = high
    out[depth + 1] = (master[...] - high.astype(jnp.float32)).astype(jnp.bfloat16)
    out[depth + 2] = first[...].astype(jnp.bfloat16)
    out[depth + 3] = second[...].astype(jnp.bfloat16)


def column_sum(column, grad, piece):
    depth = column.shape[0]
    total = column[0, 0:depth].astype(jnp.float32)
    for src in range(1, depth):
        total += column[src, 0:depth].astype(jnp.float32)
    grad[...] = total
    squares = jnp.sum(total * total, axis=0)
    squares = jnp.sum(jnp.sum(squares, axis=0, keepdims=True), axis=1, keepdims=True)
    piece[...] = jnp.broadcast_to(squares[None], piece.shape)


def advance(scale, grad, master, first_moment, second_moment):
    clipped = scale * grad
    new_first = 0.9 * first_moment + 0.1 * clipped
    new_second = 0.999 * second_moment + 0.001 * clipped * clipped
    update = new_first / (1.0 - 0.9**20) / (jnp.sqrt(new_second / (1.0 - 0.999**20)) + 1e-08)
    new_master = master - 0.0001 * (update + 0.01 * master)
    return update, new_master, new_first, new_second


def plane_update(pieces, grad, column, out, scale_out):
    depth = column.shape[0]
    squares = jnp.sum(pieces[...], axis=0)[0:1, 0:1]
    scale = jnp.minimum(1.0, 1.0 / (jnp.sqrt(squares) + 1e-06))
    scale_out[...] = jnp.broadcast_to(scale, scale_out.shape)
    high, low, first, second = (column[:, depth + i].astype(jnp.float32) for i in range(4))
    new_master = advance(scale[None], grad[...], high + low, first, second)[1]
    block = new_master.astype(jnp.bfloat16)
    for peer in range(out.shape[0]):
        out[peer] = block


def place(core, source, *refs):
    out, sems = refs[-2:]
    copies = [
        pltpu.make_async_copy(source.at[:, z], out.at[z, :, core[0]], sems.at[z])
        for z in range(out.shape[0])
    ]
    for copy in copies:
        copy.start()
    for copy in copies:
        copy.wait()


SMEM = pl.BlockSpec(memory_space=pltpu.SMEM)
ANY = pl.BlockSpec(memory_space=pl.ANY)


def local(kernel, out_shape, count, out_specs=VMEM, scratch=()):
    return pl.pallas_call(
        kernel,
        out_shape=out_shape,
        in_specs=[VMEM] * count,
        out_specs=out_specs,
        scratch_shapes=list(scratch),
        compiler_params=pltpu.CompilerParams(vmem_limit_bytes=LIMIT),
        name=kernel.__name__,
    )


def put_half(core, half, whole=None):
    peers, depth, *tile = half.shape
    size = half.size * half.dtype.itemsize
    return pl.pallas_call(
        place,
        out_shape=jax.ShapeDtypeStruct((depth, peers, 2, *tile), half.dtype),
        in_specs=[SMEM, VMEM] + [ANY] * (whole is not None),
        out_specs=ANY,
        scratch_shapes=[pltpu.SemaphoreType.DMA((depth,))],
        input_output_aliases={2: 0} if whole is not None else {},
        compiler_params=pltpu.CompilerParams(vmem_limit_bytes=LIMIT),
        cost_estimate=pl.CostEstimate(flops=0, transcendentals=0, bytes_accessed=2 * size),
        name="put_half",
    )(core, half, *(() if whole is None else (whole,)))


def exchange(value, axes):
    return lax.all_to_all(value, axes, 0, 0, tiled=False)


def to_rows(shard):
    taps = shard.shape[0]
    return shard.reshape(taps, -1, LANES).transpose(1, 0, 2).reshape(-1, LANES)


def from_rows(rows, taps):
    return rows.reshape(-1, taps, LANES).transpose(1, 0, 2).reshape(taps, -1)


def body(
    inputs, weights, ln_gain, ln_bias, projection, targets, master, first_moment, second_moment
):
    depth, plane = lax.axis_size("z"), lax.axis_size(PLANE)
    taps, width = weights.shape[0], ln_gain.shape[0]
    tile = (taps * width // LANES, LANES)
    f32, bf16 = jnp.float32, jnp.bfloat16
    shape = jax.ShapeDtypeStruct
    windows, dpre, input_grad = local_pass(inputs, weights, ln_gain, ln_bias, projection, targets)
    term = jnp.einsum("bfo,bfki->koi", dpre, windows, preferred_element_type=f32).astype(bf16)
    term = term.reshape(taps, depth, plane, width).transpose(2, 0, 1, 3)
    shards = [to_rows(value) for value in (master, first_moment, second_moment)]
    packed = local(
        plane_sum, shape((depth + 4,) + tile, bf16), 4, VMEM, (pltpu.VMEM((depth,) + tile, f32),)
    )(exchange(term, PLANE), *shards)
    column = lax.all_gather(packed, "z")
    grad, piece = local(
        column_sum,
        (shape((depth,) + tile, f32), shape((plane, 8, LANES), f32)),
        1,
        (VMEM, VMEM),
    )(column)
    pieces, input_grad = lax.optimization_barrier((exchange(piece, PLANE), input_grad))
    rows, scale = local(
        plane_update,
        (shape((plane // 2, depth) + tile, bf16), shape((8, LANES), f32)),
        3,
        (VMEM, VMEM),
    )(pieces, grad, column)
    grad = lax.dynamic_index_in_dim(grad, lax.axis_index("z"), 0, keepdims=False)
    fresh = [from_rows(value, taps) for value in advance(scale, grad, *shards)]
    update, new_master, new_first, new_second = fresh
    own = exchange(rows, PLANE[:2])
    other = lax.ppermute(own, "core", [(0, 1), (1, 0)])
    core = lax.axis_index("core").reshape(1)
    whole = put_half(core, own)
    whole = put_half(1 - core, other, whole)
    new_weights = from_rows(whole, taps)
    return (input_grad, update, new_master, new_first, new_second, new_weights)


def solution(mesh):
    grid = Mesh(mesh.devices.reshape(16, 4, 4, 2), AXES)
    return jax.shard_map(
        body,
        mesh=grid,
        in_specs=(
            P(AXES, None, None),
            P(),
            P(),
            P(),
            P(),
            P(AXES, None),
            P(None, AXES),
            P(None, AXES),
            P(None, AXES),
        ),
        out_specs=(
            P(AXES, None, None),
            P(None, AXES),
            P(None, AXES),
            P(None, AXES),
            P(None, AXES),
            P(),
        ),
        check_vma=False,
    )
```

```python
import math

import jax
import jax.numpy as jnp
from jax import lax
from jax.experimental import pallas as pl
from jax.experimental.pallas import tpu as pltpu
from jax.sharding import Mesh
from jax.sharding import PartitionSpec as P


AXES = ("z", "x", "y", "core")
PLANE = ("x", "y", "core")
SWAP = ((0, 1), (1, 0))
LANES = 128
LIMIT = 4 * 2**20
VMEM = pl.BlockSpec(memory_space=pltpu.VMEM)


def chunks(frames):
    return [slice(start, min(start + 8, frames)) for start in range(0, frames, 8)]


def middle(pre, gain, bias, projection, targets, dpre, normed, slope, deviation):
    clips, frames, width = pre.shape
    gains, biases = gain[...][None], bias[...][None]
    pooled = jnp.zeros((clips, width), jnp.float32)
    for rows in chunks(frames):
        value = pre[:, rows, :]
        center = value - jnp.mean(value, axis=-1, keepdims=True)
        spread = jnp.mean(center * center, axis=-1, keepdims=True)
        inverse = lax.rsqrt(spread + 1e-05)
        normal = center * inverse
        point = normal * gains + biases
        share = 0.5 + 0.5 * lax.erf(point * math.sqrt(0.5))
        bell = jnp.exp(-0.5 * point * point) * (1.0 / math.sqrt(2.0 * math.pi))
        pooled += jnp.sum(point * share, axis=1)
        normed[:, rows, :] = normal
        slope[:, rows, :] = (share + point * bell) * gains
        deviation[:, rows, :] = jnp.broadcast_to(inverse, inverse.shape[:2] + (LANES,))
    pooled = (pooled / frames).astype(jnp.bfloat16)
    predicted = jnp.dot(pooled, projection[...], preferred_element_type=jnp.float32)
    miss = (predicted - targets[...]).astype(jnp.bfloat16)
    back = lax.dot_general(
        miss, projection[...], (((1,), (1,)), ((), ())), preferred_element_type=jnp.float32
    )
    upstream = (back / frames)[:, None, :]
    for rows in chunks(frames):
        normal = normed[:, rows, :]
        grad = slope[:, rows, :] * upstream
        first = jnp.mean(grad, axis=-1, keepdims=True)
        second = jnp.mean(grad * normal, axis=-1, keepdims=True)
        inverse = deviation[:, rows, 0:1]
        dpre[:, rows, :] = (inverse * (grad - first - normal * second)).astype(jnp.bfloat16)


def local_pass(inputs, weights, ln_gain, ln_bias, projection, targets):
    clips, frames_in, chans = inputs.shape
    taps = weights.shape[0]
    frames_out = (frames_in - taps) // taps + 1
    windows = inputs[:, : frames_out * taps].reshape(clips, frames_out, taps, chans)
    kernel = weights.reshape(taps, chans, chans)
    pre = jnp.einsum("bfki,koi->bfo", windows, kernel, preferred_element_type=jnp.float32)
    dpre = local(
        middle,
        jax.ShapeDtypeStruct(pre.shape, jnp.bfloat16),
        5,
        VMEM,
        (
            pltpu.VMEM(pre.shape, jnp.float32),
            pltpu.VMEM(pre.shape, jnp.float32),
            pltpu.VMEM(pre.shape[:2] + (LANES,), jnp.float32),
        ),
    )(pre, ln_gain[None], ln_bias[None], projection, targets)
    dwin = jnp.einsum("bfo,koi->bfki", dpre, kernel, preferred_element_type=jnp.float32).astype(
        jnp.bfloat16
    )
    dinput = dwin.reshape(clips, frames_out * taps, chans)
    tail = jnp.zeros((clips, frames_in - frames_out * taps, chans), jnp.bfloat16)
    return (windows, dpre, jnp.concatenate([dinput, tail], axis=1))


def merge(core, term, recv, out):
    for peer in range(out.shape[0]):
        total = term[peer, core[0]].astype(jnp.float32) + recv[peer].astype(jnp.float32)
        out[peer] = total.astype(jnp.bfloat16)


def plane_sum(recv, master, first, second, out, rows):
    peers, taps, depth, width = recv.shape
    parts = width // LANES
    for tap in range(taps):
        total = recv[0, tap].astype(jnp.float32)
        for src in range(1, peers):
            total += recv[src, tap].astype(jnp.float32)
        for part in range(parts):
            rows[:, part * taps + tap, :] = total[:, part * LANES : (part + 1) * LANES]
    out[0:depth] = rows[...].astype(jnp.bfloat16)
    high = master[...].astype(jnp.bfloat16)
    out[depth] = high
    out[depth + 1] = (master[...] - high.astype(jnp.float32)).astype(jnp.bfloat16)
    out[depth + 2] = first[...].astype(jnp.bfloat16)
    out[depth + 3] = second[...].astype(jnp.bfloat16)


def column_sum(column, grad, piece):
    depth = column.shape[0]
    total = column[0, 0:depth].astype(jnp.float32)
    for src in range(1, depth):
        total += column[src, 0:depth].astype(jnp.float32)
    grad[...] = total
    squares = jnp.sum(total * total, axis=0)
    squares = jnp.sum(jnp.sum(squares, axis=0, keepdims=True), axis=1, keepdims=True)
    piece[...] = jnp.broadcast_to(squares[None], piece.shape)


def advance(scale, grad, master, first_moment, second_moment):
    clipped = scale * grad
    new_first = 0.9 * first_moment + 0.1 * clipped
    new_second = 0.999 * second_moment + 0.001 * clipped * clipped
    update = new_first / (1.0 - 0.9**20) / (jnp.sqrt(new_second / (1.0 - 0.999**20)) + 1e-08)
    new_master = master - 0.0001 * (update + 0.01 * master)
    return update, new_master, new_first, new_second


def plane_update(pieces, grad, column, out, scale_out):
    depth = column.shape[0]
    squares = jnp.sum(pieces[...], axis=0)[0:1, 0:1]
    scale = jnp.minimum(1.0, 1.0 / (jnp.sqrt(squares) + 1e-06))
    scale_out[...] = jnp.broadcast_to(scale, scale_out.shape)
    high, low, first, second = (column[:, depth + i].astype(jnp.float32) for i in range(4))
    new_master = advance(scale[None], grad[...], high + low, first, second)[1]
    block = new_master.astype(jnp.bfloat16)
    for peer in range(out.shape[0]):
        out[peer] = block


def place(core, source, *refs):
    out, sems = refs[-2:]
    copies = [
        pltpu.make_async_copy(source.at[:, z], out.at[z, :, core[0]], sems.at[z])
        for z in range(out.shape[0])
    ]
    for copy in copies:
        copy.start()
    for copy in copies:
        copy.wait()


SMEM = pl.BlockSpec(memory_space=pltpu.SMEM)
ANY = pl.BlockSpec(memory_space=pl.ANY)


def local(kernel, out_shape, count, out_specs=VMEM, scratch=()):
    return pl.pallas_call(
        kernel,
        out_shape=out_shape,
        in_specs=[VMEM] * count,
        out_specs=out_specs,
        scratch_shapes=list(scratch),
        compiler_params=pltpu.CompilerParams(vmem_limit_bytes=LIMIT),
        name=kernel.__name__,
    )


def put_half(core, half, whole=None):
    peers, depth, *tile = half.shape
    size = half.size * half.dtype.itemsize
    return pl.pallas_call(
        place,
        out_shape=jax.ShapeDtypeStruct((depth, peers, 2, *tile), half.dtype),
        in_specs=[SMEM, VMEM] + [ANY] * (whole is not None),
        out_specs=ANY,
        scratch_shapes=[pltpu.SemaphoreType.DMA((depth,))],
        input_output_aliases={2: 0} if whole is not None else {},
        compiler_params=pltpu.CompilerParams(vmem_limit_bytes=LIMIT),
        cost_estimate=pl.CostEstimate(flops=0, transcendentals=0, bytes_accessed=2 * size),
        name="put_half",
    )(core, half, *(() if whole is None else (whole,)))


def exchange(value, axes):
    return lax.all_to_all(value, axes, 0, 0, tiled=False)


def to_rows(shard):
    taps = shard.shape[0]
    return shard.reshape(taps, -1, LANES).transpose(1, 0, 2).reshape(-1, LANES)


def from_rows(rows, taps):
    return rows.reshape(-1, taps, LANES).transpose(1, 0, 2).reshape(taps, -1)


def body(
    inputs, weights, ln_gain, ln_bias, projection, targets, master, first_moment, second_moment
):
    depth, plane = lax.axis_size("z"), lax.axis_size(PLANE)
    taps, width = weights.shape[0], ln_gain.shape[0]
    tile = (taps * width // LANES, LANES)
    f32, bf16 = jnp.float32, jnp.bfloat16
    shape = jax.ShapeDtypeStruct
    windows, dpre, input_grad = local_pass(inputs, weights, ln_gain, ln_bias, projection, targets)
    term = jnp.einsum("bfo,bfki->koi", dpre, windows, preferred_element_type=f32).astype(bf16)
    term = term.reshape(taps, depth, plane, width).transpose(2, 0, 1, 3)
    term = lax.optimization_barrier(term).reshape(plane // 2, 2, taps, depth, width)
    core = lax.axis_index("core").reshape(1)
    away = lax.dynamic_index_in_dim(term, 1 - core[0], 1, keepdims=False)
    term = pl.pallas_call(
        merge,
        out_shape=shape(away.shape, bf16),
        in_specs=[SMEM, VMEM, VMEM],
        out_specs=VMEM,
        compiler_params=pltpu.CompilerParams(vmem_limit_bytes=LIMIT),
        name="merge",
    )(core, term, lax.ppermute(away, "core", SWAP))
    shards = [to_rows(value) for value in (master, first_moment, second_moment)]
    packed = local(
        plane_sum, shape((depth + 4,) + tile, bf16), 4, VMEM, (pltpu.VMEM((depth,) + tile, f32),)
    )(exchange(term, PLANE[:2]), *shards)
    column = lax.all_gather(packed, "z")
    grad, piece = local(
        column_sum,
        (shape((depth,) + tile, f32), shape((plane, 8, LANES), f32)),
        1,
        (VMEM, VMEM),
    )(column)
    pieces, input_grad = lax.optimization_barrier((exchange(piece, PLANE), input_grad))
    rows, scale = local(
        plane_update,
        (shape((plane // 2, depth) + tile, bf16), shape((8, LANES), f32)),
        3,
        (VMEM, VMEM),
    )(pieces, grad, column)
    grad = lax.dynamic_index_in_dim(grad, lax.axis_index("z"), 0, keepdims=False)
    fresh = [from_rows(value, taps) for value in advance(scale, grad, *shards)]
    update, new_master, new_first, new_second = fresh
    own = exchange(rows, PLANE[:2])
    other = lax.ppermute(own, "core", SWAP)
    whole = put_half(core, own)
    whole = put_half(1 - core, other, whole)
    new_weights = from_rows(whole, taps)
    return (input_grad, update, new_master, new_first, new_second, new_weights)


def solution(mesh):
    grid = Mesh(mesh.devices.reshape(16, 4, 4, 2), AXES)
    return jax.shard_map(
        body,
        mesh=grid,
        in_specs=(
            P(AXES, None, None),
            P(),
            P(),
            P(),
            P(),
            P(AXES, None),
            P(None, AXES),
            P(None, AXES),
            P(None, AXES),
        ),
        out_specs=(
            P(AXES, None, None),
            P(None, AXES),
            P(None, AXES),
            P(None, AXES),
            P(None, AXES),
            P(),
        ),
        check_vma=False,
    )
```

```python
import math

import jax
import jax.numpy as jnp
from jax import lax
from jax.experimental import pallas as pl
from jax.experimental.pallas import tpu as pltpu
from jax.sharding import Mesh
from jax.sharding import PartitionSpec as P


AXES = ("z", "x", "y", "core")
PLANE = ("x", "y", "core")
SWAP = ((0, 1), (1, 0))
LANES = 128
LIMIT = 4 * 2**20
VMEM = pl.BlockSpec(memory_space=pltpu.VMEM)


def chunks(frames):
    return [slice(start, min(start + 8, frames)) for start in range(0, frames, 8)]


def middle(pre, gain, bias, projection, targets, dpre, normed, slope, deviation):
    clips, frames, width = pre.shape
    gains, biases = gain[...][None], bias[...][None]
    pooled = jnp.zeros((clips, width), jnp.float32)
    for rows in chunks(frames):
        value = pre[:, rows, :]
        center = value - jnp.mean(value, axis=-1, keepdims=True)
        spread = jnp.mean(center * center, axis=-1, keepdims=True)
        inverse = lax.rsqrt(spread + 1e-05)
        normal = center * inverse
        point = normal * gains + biases
        share = 0.5 + 0.5 * lax.erf(point * math.sqrt(0.5))
        bell = jnp.exp(-0.5 * point * point) * (1.0 / math.sqrt(2.0 * math.pi))
        pooled += jnp.sum(point * share, axis=1)
        normed[:, rows, :] = normal
        slope[:, rows, :] = (share + point * bell) * gains
        deviation[:, rows, :] = jnp.broadcast_to(inverse, inverse.shape[:2] + (LANES,))
    pooled = (pooled / frames).astype(jnp.bfloat16)
    predicted = jnp.dot(pooled, projection[...], preferred_element_type=jnp.float32)
    miss = (predicted - targets[...]).astype(jnp.bfloat16)
    back = lax.dot_general(
        miss, projection[...], (((1,), (1,)), ((), ())), preferred_element_type=jnp.float32
    )
    upstream = (back / frames)[:, None, :]
    for rows in chunks(frames):
        normal = normed[:, rows, :]
        grad = slope[:, rows, :] * upstream
        first = jnp.mean(grad, axis=-1, keepdims=True)
        second = jnp.mean(grad * normal, axis=-1, keepdims=True)
        inverse = deviation[:, rows, 0:1]
        dpre[:, rows, :] = (inverse * (grad - first - normal * second)).astype(jnp.bfloat16)


def local_pass(inputs, weights, ln_gain, ln_bias, projection, targets):
    clips, frames_in, chans = inputs.shape
    taps = weights.shape[0]
    frames_out = (frames_in - taps) // taps + 1
    windows = inputs[:, : frames_out * taps].reshape(clips, frames_out, taps, chans)
    kernel = weights.reshape(taps, chans, chans)
    pre = jnp.einsum("bfki,koi->bfo", windows, kernel, preferred_element_type=jnp.float32)
    dpre = local(
        middle,
        jax.ShapeDtypeStruct(pre.shape, jnp.bfloat16),
        5,
        VMEM,
        (
            pltpu.VMEM(pre.shape, jnp.float32),
            pltpu.VMEM(pre.shape, jnp.float32),
            pltpu.VMEM(pre.shape[:2] + (LANES,), jnp.float32),
        ),
    )(pre, ln_gain[None], ln_bias[None], projection, targets)
    dwin = jnp.einsum("bfo,koi->bfki", dpre, kernel, preferred_element_type=jnp.float32).astype(
        jnp.bfloat16
    )
    dinput = dwin.reshape(clips, frames_out * taps, chans)
    tail = jnp.zeros((clips, frames_in - frames_out * taps, chans), jnp.bfloat16)
    return (windows, dpre, jnp.concatenate([dinput, tail], axis=1))


def merge(core, term, recv, out):
    for peer in range(out.shape[0]):
        total = term[peer, core[0]].astype(jnp.float32) + recv[peer].astype(jnp.float32)
        out[peer] = total.astype(jnp.bfloat16)


def plane_sum(recv, master, first, second, out, rows):
    peers, taps, depth, width = recv.shape
    parts = width // LANES
    for tap in range(taps):
        total = recv[0, tap].astype(jnp.float32)
        for src in range(1, peers):
            total += recv[src, tap].astype(jnp.float32)
        for part in range(parts):
            rows[:, part * taps + tap, :] = total[:, part * LANES : (part + 1) * LANES]
    out[0:depth] = rows[...].astype(jnp.bfloat16)
    high = master[...].astype(jnp.bfloat16)
    out[depth] = high
    out[depth + 1] = (master[...] - high.astype(jnp.float32)).astype(jnp.bfloat16)
    out[depth + 2] = first[...].astype(jnp.bfloat16)
    out[depth + 3] = second[...].astype(jnp.bfloat16)


def column_sum(column, grad, piece):
    depth = column.shape[0]
    total = column[0, 0:depth].astype(jnp.float32)
    for src in range(1, depth):
        total += column[src, 0:depth].astype(jnp.float32)
    grad[...] = total
    squares = jnp.sum(total * total, axis=0)
    squares = jnp.sum(jnp.sum(squares, axis=0, keepdims=True), axis=1, keepdims=True)
    piece[...] = jnp.broadcast_to(squares[None], piece.shape)


def advance(scale, grad, master, first_moment, second_moment):
    clipped = scale * grad
    new_first = 0.9 * first_moment + 0.1 * clipped
    new_second = 0.999 * second_moment + 0.001 * clipped * clipped
    update = new_first / (1.0 - 0.9**20) / (jnp.sqrt(new_second / (1.0 - 0.999**20)) + 1e-08)
    new_master = master - 0.0001 * (update + 0.01 * master)
    return update, new_master, new_first, new_second


def plane_update(pieces, grad, column, out, scale_out):
    depth = column.shape[0]
    squares = jnp.sum(pieces[...], axis=0)[0:1, 0:1]
    scale = jnp.minimum(1.0, 1.0 / (jnp.sqrt(squares) + 1e-06))
    scale_out[...] = jnp.broadcast_to(scale, scale_out.shape)
    high, low, first, second = (column[:, depth + i].astype(jnp.float32) for i in range(4))
    new_master = advance(scale[None], grad[...], high + low, first, second)[1]
    block = new_master.astype(jnp.bfloat16)
    for peer in range(out.shape[0]):
        out[peer] = block


def place(core, source, *refs):
    out, sems = refs[-2:]
    copies = [
        pltpu.make_async_copy(source.at[:, z], out.at[z, :, core[0]], sems.at[z])
        for z in range(out.shape[0])
    ]
    for copy in copies:
        copy.start()
    for copy in copies:
        copy.wait()


SMEM = pl.BlockSpec(memory_space=pltpu.SMEM)
ANY = pl.BlockSpec(memory_space=pl.ANY)


def local(kernel, out_shape, count, out_specs=VMEM, scratch=()):
    return pl.pallas_call(
        kernel,
        out_shape=out_shape,
        in_specs=[VMEM] * count,
        out_specs=out_specs,
        scratch_shapes=list(scratch),
        compiler_params=pltpu.CompilerParams(vmem_limit_bytes=LIMIT),
        name=kernel.__name__,
    )


def put_half(core, half, whole=None):
    peers, depth, *tile = half.shape
    size = half.size * half.dtype.itemsize
    return pl.pallas_call(
        place,
        out_shape=jax.ShapeDtypeStruct((depth, peers, 2, *tile), half.dtype),
        in_specs=[SMEM, VMEM] + [ANY] * (whole is not None),
        out_specs=ANY,
        scratch_shapes=[pltpu.SemaphoreType.DMA((depth,))],
        input_output_aliases={2: 0} if whole is not None else {},
        compiler_params=pltpu.CompilerParams(vmem_limit_bytes=LIMIT),
        cost_estimate=pl.CostEstimate(flops=0, transcendentals=0, bytes_accessed=2 * size),
        name="put_half",
    )(core, half, *(() if whole is None else (whole,)))


def exchange(value, axes):
    return lax.all_to_all(value, axes, 0, 0, tiled=False)


def to_rows(shard):
    taps = shard.shape[0]
    return shard.reshape(taps, -1, LANES).transpose(1, 0, 2).reshape(-1, LANES)


def from_rows(rows, taps):
    return rows.reshape(-1, taps, LANES).transpose(1, 0, 2).reshape(taps, -1)


def body(
    inputs, weights, ln_gain, ln_bias, projection, targets, master, first_moment, second_moment
):
    depth, plane = lax.axis_size("z"), lax.axis_size(PLANE)
    taps, width = weights.shape[0], ln_gain.shape[0]
    tile = (taps * width // LANES, LANES)
    f32, bf16 = jnp.float32, jnp.bfloat16
    shape = jax.ShapeDtypeStruct
    windows, dpre, input_grad = local_pass(inputs, weights, ln_gain, ln_bias, projection, targets)
    term = jnp.einsum("bfo,bfki->koi", dpre, windows, preferred_element_type=f32).astype(bf16)
    term = term.reshape(taps, depth, plane, width).transpose(2, 0, 1, 3)
    term = lax.optimization_barrier(term).reshape(plane // 2, 2, taps, depth, width)
    core = lax.axis_index("core").reshape(1)
    away = lax.dynamic_index_in_dim(term, 1 - core[0], 1, keepdims=False)
    recv = lax.ppermute(away, "core", SWAP)
    recv, input_grad = lax.optimization_barrier((recv, input_grad))
    term = pl.pallas_call(
        merge,
        out_shape=shape(away.shape, bf16),
        in_specs=[SMEM, VMEM, VMEM],
        out_specs=VMEM,
        compiler_params=pltpu.CompilerParams(vmem_limit_bytes=LIMIT),
        name="merge",
    )(core, term, recv)
    shards = [to_rows(value) for value in (master, first_moment, second_moment)]
    packed = local(
        plane_sum, shape((depth + 4,) + tile, bf16), 4, VMEM, (pltpu.VMEM((depth,) + tile, f32),)
    )(exchange(term, PLANE[:2]), *shards)
    column = lax.all_gather(packed, "z")
    grad, piece = local(
        column_sum,
        (shape((depth,) + tile, f32), shape((plane, 8, LANES), f32)),
        1,
        (VMEM, VMEM),
    )(column)
    rows, scale = local(
        plane_update,
        (shape((plane // 2, depth) + tile, bf16), shape((8, LANES), f32)),
        3,
        (VMEM, VMEM),
    )(exchange(piece, PLANE), grad, column)
    grad = lax.dynamic_index_in_dim(grad, lax.axis_index("z"), 0, keepdims=False)
    fresh = [from_rows(value, taps) for value in advance(scale, grad, *shards)]
    update, new_master, new_first, new_second = fresh
    own = exchange(rows, PLANE[:2])
    other = lax.ppermute(own, "core", SWAP)
    whole = put_half(core, own)
    whole = put_half(1 - core, other, whole)
    new_weights = from_rows(whole, taps)
    return (input_grad, update, new_master, new_first, new_second, new_weights)


def solution(mesh):
    grid = Mesh(mesh.devices.reshape(16, 4, 4, 2), AXES)
    return jax.shard_map(
        body,
        mesh=grid,
        in_specs=(
            P(AXES, None, None),
            P(),
            P(),
            P(),
            P(),
            P(AXES, None),
            P(None, AXES),
            P(None, AXES),
            P(None, AXES),
        ),
        out_specs=(
            P(AXES, None, None),
            P(None, AXES),
            P(None, AXES),
            P(None, AXES),
            P(None, AXES),
            P(),
        ),
        check_vma=False,
    )
```

```python
import math

import jax
import jax.numpy as jnp
from jax import lax
from jax.experimental import pallas as pl
from jax.experimental.pallas import tpu as pltpu
from jax.sharding import Mesh
from jax.sharding import PartitionSpec as P


AXES = ("z", "x", "y", "core")
PLANE = ("x", "y", "core")
SWAP = ((0, 1), (1, 0))
LANES = 128
LIMIT = 4 * 2**20
VMEM = pl.BlockSpec(memory_space=pltpu.VMEM)


def chunks(frames):
    return [slice(start, min(start + 8, frames)) for start in range(0, frames, 8)]


def forward(pre, gain, bias, normed, slope, deviation, pool):
    clips, frames, width = pre.shape
    gains, biases = gain[...][None], bias[...][None]
    pooled = jnp.zeros((clips, width), jnp.float32)
    for rows in chunks(frames):
        value = pre[:, rows, :]
        center = value - jnp.mean(value, axis=-1, keepdims=True)
        spread = jnp.mean(center * center, axis=-1, keepdims=True)
        inverse = lax.rsqrt(spread + 1e-05)
        normal = center * inverse
        point = normal * gains + biases
        share = 0.5 + 0.5 * lax.erf(point * math.sqrt(0.5))
        bell = jnp.exp(-0.5 * point * point) * (1.0 / math.sqrt(2.0 * math.pi))
        pooled += jnp.sum(point * share, axis=1)
        normed[:, rows, :] = normal
        slope[:, rows, :] = (share + point * bell) * gains
        deviation[:, rows, :] = jnp.broadcast_to(inverse, inverse.shape[:2] + (LANES,))
    pool[...] = (pooled / frames).astype(jnp.bfloat16)


def backward(normed, slope, deviation, pool, projection, targets, dpre):
    frames = dpre.shape[1]
    predicted = jnp.dot(pool[...], projection[...], preferred_element_type=jnp.float32)
    miss = (predicted - targets[...]).astype(jnp.bfloat16)
    back = lax.dot_general(
        miss, projection[...], (((1,), (1,)), ((), ())), preferred_element_type=jnp.float32
    )
    upstream = (back / frames)[:, None, :]
    for rows in chunks(frames):
        normal = normed[:, rows, :]
        grad = slope[:, rows, :] * upstream
        first = jnp.mean(grad, axis=-1, keepdims=True)
        second = jnp.mean(grad * normal, axis=-1, keepdims=True)
        inverse = deviation[:, rows, 0:1]
        dpre[:, rows, :] = (inverse * (grad - first - normal * second)).astype(jnp.bfloat16)


def local_pass(inputs, weights, ln_gain, ln_bias, projection, targets):
    clips, frames_in, chans = inputs.shape
    taps = weights.shape[0]
    frames_out = (frames_in - taps) // taps + 1
    windows = inputs[:, : frames_out * taps].reshape(clips, frames_out, taps, chans)
    kernel = weights.reshape(taps, chans, chans)
    pre = jnp.einsum("bfki,koi->bfo", windows, kernel, preferred_element_type=jnp.float32)
    shape, f32, bf16 = jax.ShapeDtypeStruct, jnp.float32, jnp.bfloat16
    saved = local(
        forward,
        (
            shape(pre.shape, f32),
            shape(pre.shape, f32),
            shape(pre.shape[:2] + (LANES,), f32),
            shape((clips, chans), bf16),
        ),
        3,
        (VMEM,) * 4,
    )(pre, ln_gain[None], ln_bias[None])
    dpre = local(backward, shape(pre.shape, bf16), 6)(*saved, projection, targets)
    dwin = jnp.einsum("bfo,koi->bfki", dpre, kernel, preferred_element_type=jnp.float32).astype(
        jnp.bfloat16
    )
    dinput = dwin.reshape(clips, frames_out * taps, chans)
    tail = jnp.zeros((clips, frames_in - frames_out * taps, chans), jnp.bfloat16)
    return (windows, dpre, jnp.concatenate([dinput, tail], axis=1))


def merge(core, term, recv, out):
    for peer in range(out.shape[0]):
        total = term[peer, core[0]].astype(jnp.float32) + recv[peer].astype(jnp.float32)
        out[peer] = total.astype(jnp.bfloat16)


def plane_sum(recv, master, first, second, out, rows):
    peers, taps, depth, width = recv.shape
    parts = width // LANES
    for tap in range(taps):
        total = recv[0, tap].astype(jnp.float32)
        for src in range(1, peers):
            total += recv[src, tap].astype(jnp.float32)
        for part in range(parts):
            rows[:, part * taps + tap, :] = total[:, part * LANES : (part + 1) * LANES]
    out[0:depth] = rows[...].astype(jnp.bfloat16)
    high = master[...].astype(jnp.bfloat16)
    out[depth] = high
    out[depth + 1] = (master[...] - high.astype(jnp.float32)).astype(jnp.bfloat16)
    out[depth + 2] = first[...].astype(jnp.bfloat16)
    out[depth + 3] = second[...].astype(jnp.bfloat16)


def column_sum(column, grad, piece):
    depth = column.shape[0]
    total = column[0, 0:depth].astype(jnp.float32)
    for src in range(1, depth):
        total += column[src, 0:depth].astype(jnp.float32)
    grad[...] = total
    squares = jnp.sum(total * total, axis=0)
    squares = jnp.sum(jnp.sum(squares, axis=0, keepdims=True), axis=1, keepdims=True)
    piece[...] = jnp.broadcast_to(squares[None], piece.shape)


def advance(scale, grad, master, first_moment, second_moment):
    clipped = scale * grad
    new_first = 0.9 * first_moment + 0.1 * clipped
    new_second = 0.999 * second_moment + 0.001 * clipped * clipped
    update = new_first / (1.0 - 0.9**20) / (jnp.sqrt(new_second / (1.0 - 0.999**20)) + 1e-08)
    new_master = master - 0.0001 * (update + 0.01 * master)
    return update, new_master, new_first, new_second


def plane_update(pieces, grad, column, out, scale_out):
    depth = column.shape[0]
    squares = jnp.sum(pieces[...], axis=0)[0:1, 0:1]
    scale = jnp.minimum(1.0, 1.0 / (jnp.sqrt(squares) + 1e-06))
    scale_out[...] = jnp.broadcast_to(scale, scale_out.shape)
    high, low, first, second = (column[:, depth + i].astype(jnp.float32) for i in range(4))
    new_master = advance(scale[None], grad[...], high + low, first, second)[1]
    block = new_master.astype(jnp.bfloat16)
    for peer in range(out.shape[0]):
        out[peer] = block


def place(core, source, *refs):
    out, sems = refs[-2:]
    copies = [
        pltpu.make_async_copy(source.at[:, z], out.at[z, :, core[0]], sems.at[z])
        for z in range(out.shape[0])
    ]
    for copy in copies:
        copy.start()
    for copy in copies:
        copy.wait()


SMEM = pl.BlockSpec(memory_space=pltpu.SMEM)
ANY = pl.BlockSpec(memory_space=pl.ANY)


def local(kernel, out_shape, count, out_specs=VMEM, scratch=()):
    return pl.pallas_call(
        kernel,
        out_shape=out_shape,
        in_specs=[VMEM] * count,
        out_specs=out_specs,
        scratch_shapes=list(scratch),
        compiler_params=pltpu.CompilerParams(vmem_limit_bytes=LIMIT),
        name=kernel.__name__,
    )


def put_half(core, half, whole=None):
    peers, depth, *tile = half.shape
    size = half.size * half.dtype.itemsize
    return pl.pallas_call(
        place,
        out_shape=jax.ShapeDtypeStruct((depth, peers, 2, *tile), half.dtype),
        in_specs=[SMEM, VMEM] + [ANY] * (whole is not None),
        out_specs=ANY,
        scratch_shapes=[pltpu.SemaphoreType.DMA((depth,))],
        input_output_aliases={2: 0} if whole is not None else {},
        compiler_params=pltpu.CompilerParams(vmem_limit_bytes=LIMIT),
        cost_estimate=pl.CostEstimate(flops=0, transcendentals=0, bytes_accessed=2 * size),
        name="put_half",
    )(core, half, *(() if whole is None else (whole,)))


def exchange(value, axes):
    return lax.all_to_all(value, axes, 0, 0, tiled=False)


def to_rows(shard):
    taps = shard.shape[0]
    return shard.reshape(taps, -1, LANES).transpose(1, 0, 2).reshape(-1, LANES)


def from_rows(rows, taps):
    return rows.reshape(-1, taps, LANES).transpose(1, 0, 2).reshape(taps, -1)


def body(
    inputs, weights, ln_gain, ln_bias, projection, targets, master, first_moment, second_moment
):
    depth, plane = lax.axis_size("z"), lax.axis_size(PLANE)
    taps, width = weights.shape[0], ln_gain.shape[0]
    tile = (taps * width // LANES, LANES)
    f32, bf16 = jnp.float32, jnp.bfloat16
    shape = jax.ShapeDtypeStruct
    windows, dpre, input_grad = local_pass(inputs, weights, ln_gain, ln_bias, projection, targets)
    term = jnp.einsum("bfo,bfki->koi", dpre, windows, preferred_element_type=f32).astype(bf16)
    term = term.reshape(taps, depth, plane, width).transpose(2, 0, 1, 3)
    term = lax.optimization_barrier(term).reshape(plane // 2, 2, taps, depth, width)
    core = lax.axis_index("core").reshape(1)
    away = lax.dynamic_index_in_dim(term, 1 - core[0], 1, keepdims=False)
    recv = lax.ppermute(away, "core", SWAP)
    recv, input_grad = lax.optimization_barrier((recv, input_grad))
    term = pl.pallas_call(
        merge,
        out_shape=shape(away.shape, bf16),
        in_specs=[SMEM, VMEM, VMEM],
        out_specs=VMEM,
        compiler_params=pltpu.CompilerParams(vmem_limit_bytes=LIMIT),
        name="merge",
    )(core, term, recv)
    shards = [to_rows(value) for value in (master, first_moment, second_moment)]
    packed = local(
        plane_sum, shape((depth + 4,) + tile, bf16), 4, VMEM, (pltpu.VMEM((depth,) + tile, f32),)
    )(exchange(term, PLANE[:2]), *shards)
    column = lax.all_gather(packed, "z")
    grad, piece = local(
        column_sum,
        (shape((depth,) + tile, f32), shape((plane, 8, LANES), f32)),
        1,
        (VMEM, VMEM),
    )(column)
    rows, scale = local(
        plane_update,
        (shape((plane // 2, depth) + tile, bf16), shape((8, LANES), f32)),
        3,
        (VMEM, VMEM),
    )(exchange(piece, PLANE), grad, column)
    grad = lax.dynamic_index_in_dim(grad, lax.axis_index("z"), 0, keepdims=False)
    fresh = [from_rows(value, taps) for value in advance(scale, grad, *shards)]
    update, new_master, new_first, new_second = fresh
    own = exchange(rows, PLANE[:2])
    other = lax.ppermute(own, "core", SWAP)
    whole = put_half(core, own)
    whole = put_half(1 - core, other, whole)
    new_weights = from_rows(whole, taps)
    return (input_grad, update, new_master, new_first, new_second, new_weights)


def solution(mesh):
    grid = Mesh(mesh.devices.reshape(16, 4, 4, 2), AXES)
    return jax.shard_map(
        body,
        mesh=grid,
        in_specs=(
            P(AXES, None, None),
            P(),
            P(),
            P(),
            P(),
            P(AXES, None),
            P(None, AXES),
            P(None, AXES),
            P(None, AXES),
        ),
        out_specs=(
            P(AXES, None, None),
            P(None, AXES),
            P(None, AXES),
            P(None, AXES),
            P(None, AXES),
            P(),
        ),
        check_vma=False,
    )
```

```python
import math

import jax
import jax.numpy as jnp
from jax import lax
from jax.experimental import pallas as pl
from jax.experimental.pallas import tpu as pltpu
from jax.sharding import Mesh
from jax.sharding import PartitionSpec as P


AXES = ("z", "x", "y", "core")
PLANE = ("x", "y", "core")
SWAP = ((0, 1), (1, 0))
LANES = 128
LIMIT = 4 * 2**20
VMEM = pl.BlockSpec(memory_space=pltpu.VMEM)


def chunks(frames):
    return [slice(start, min(start + 8, frames)) for start in range(0, frames, 8)]


def forward(pre, gain, bias, normed, slope, deviation, pool):
    clips, frames, width = pre.shape
    gains, biases = gain[...][None], bias[...][None]
    pooled = jnp.zeros((clips, width), jnp.float32)
    for rows in chunks(frames):
        value = pre[:, rows, :]
        center = value - jnp.mean(value, axis=-1, keepdims=True)
        spread = jnp.mean(center * center, axis=-1, keepdims=True)
        inverse = lax.rsqrt(spread + 1e-05)
        normal = center * inverse
        point = normal * gains + biases
        share = 0.5 + 0.5 * lax.erf(point * math.sqrt(0.5))
        bell = jnp.exp(-0.5 * point * point) * (1.0 / math.sqrt(2.0 * math.pi))
        pooled += jnp.sum(point * share, axis=1)
        normed[:, rows, :] = normal
        slope[:, rows, :] = (share + point * bell) * gains
        deviation[:, rows, :] = jnp.broadcast_to(inverse, inverse.shape[:2] + (LANES,))
    pool[...] = (pooled / frames).astype(jnp.bfloat16)


def backward(normed, slope, deviation, pool, projection, targets, dpre):
    frames = dpre.shape[1]
    predicted = jnp.dot(pool[...], projection[...], preferred_element_type=jnp.float32)
    miss = (predicted - targets[...]).astype(jnp.bfloat16)
    back = lax.dot_general(
        miss, projection[...], (((1,), (1,)), ((), ())), preferred_element_type=jnp.float32
    )
    upstream = (back / frames)[:, None, :]
    for rows in chunks(frames):
        normal = normed[:, rows, :]
        grad = slope[:, rows, :] * upstream
        first = jnp.mean(grad, axis=-1, keepdims=True)
        second = jnp.mean(grad * normal, axis=-1, keepdims=True)
        inverse = deviation[:, rows, 0:1]
        dpre[:, rows, :] = (inverse * (grad - first - normal * second)).astype(jnp.bfloat16)


def with_tail(frames, out, tail, sems):
    count = frames.shape[0]
    body_copy = pltpu.make_async_copy(frames, out.at[pl.ds(0, count)], sems.at[0])
    body_copy.start()
    tail[...] = jnp.zeros_like(tail)
    tail_copy = pltpu.make_async_copy(tail, out.at[pl.ds(count, tail.shape[0])], sems.at[1])
    tail_copy.start()
    body_copy.wait()
    tail_copy.wait()


def local_pass(inputs, weights, ln_gain, ln_bias, projection, targets):
    clips, frames_in, chans = inputs.shape
    taps = weights.shape[0]
    frames_out = (frames_in - taps) // taps + 1
    windows = inputs[:, : frames_out * taps].reshape(clips, frames_out, taps, chans)
    kernel = weights.reshape(taps, chans, chans)
    pre = jnp.einsum("bfki,koi->bfo", windows, kernel, preferred_element_type=jnp.float32)
    shape, f32, bf16 = jax.ShapeDtypeStruct, jnp.float32, jnp.bfloat16
    saved = local(
        forward,
        (
            shape(pre.shape, f32),
            shape(pre.shape, f32),
            shape(pre.shape[:2] + (LANES,), f32),
            shape((clips, chans), bf16),
        ),
        3,
        (VMEM,) * 4,
    )(pre, ln_gain[None], ln_bias[None])
    dpre = local(backward, shape(pre.shape, bf16), 6)(*saved, projection, targets)
    dwin = jnp.einsum("bfo,koi->bfki", dpre, kernel, preferred_element_type=jnp.float32).astype(
        jnp.bfloat16
    )
    dinput = dwin.reshape(clips, frames_out * taps, chans).transpose(1, 0, 2)
    rest = frames_in - frames_out * taps
    dinput = pl.pallas_call(
        with_tail,
        out_shape=shape((frames_in, clips, chans), bf16),
        in_specs=[VMEM],
        out_specs=pl.BlockSpec(memory_space=pl.ANY),
        scratch_shapes=[pltpu.VMEM((rest, clips, chans), bf16), pltpu.SemaphoreType.DMA((2,))],
        compiler_params=pltpu.CompilerParams(vmem_limit_bytes=LIMIT),
        name="with_tail",
    )(dinput)
    return (windows, dpre, dinput.transpose(1, 0, 2))


def merge(core, term, recv, out):
    for peer in range(out.shape[0]):
        total = term[peer, core[0]].astype(jnp.float32) + recv[peer].astype(jnp.float32)
        out[peer] = total.astype(jnp.bfloat16)


def plane_sum(recv, master, first, second, out, rows):
    peers, taps, depth, width = recv.shape
    parts = width // LANES
    for tap in range(taps):
        total = recv[0, tap].astype(jnp.float32)
        for src in range(1, peers):
            total += recv[src, tap].astype(jnp.float32)
        for part in range(parts):
            rows[:, part * taps + tap, :] = total[:, part * LANES : (part + 1) * LANES]
    out[0:depth] = rows[...].astype(jnp.bfloat16)
    high = master[...].astype(jnp.bfloat16)
    out[depth] = high
    out[depth + 1] = (master[...] - high.astype(jnp.float32)).astype(jnp.bfloat16)
    out[depth + 2] = first[...].astype(jnp.bfloat16)
    out[depth + 3] = second[...].astype(jnp.bfloat16)


def column_sum(column, grad, piece):
    depth = column.shape[0]
    total = column[0, 0:depth].astype(jnp.float32)
    for src in range(1, depth):
        total += column[src, 0:depth].astype(jnp.float32)
    grad[...] = total
    squares = jnp.sum(total * total, axis=0)
    squares = jnp.sum(jnp.sum(squares, axis=0, keepdims=True), axis=1, keepdims=True)
    piece[...] = jnp.broadcast_to(squares[None], piece.shape)


def advance(scale, grad, master, first_moment, second_moment):
    clipped = scale * grad
    new_first = 0.9 * first_moment + 0.1 * clipped
    new_second = 0.999 * second_moment + 0.001 * clipped * clipped
    update = new_first / (1.0 - 0.9**20) / (jnp.sqrt(new_second / (1.0 - 0.999**20)) + 1e-08)
    new_master = master - 0.0001 * (update + 0.01 * master)
    return update, new_master, new_first, new_second


def plane_update(pieces, grad, column, out, scale_out):
    depth = column.shape[0]
    squares = jnp.sum(pieces[...], axis=0)[0:1, 0:1]
    scale = jnp.minimum(1.0, 1.0 / (jnp.sqrt(squares) + 1e-06))
    scale_out[...] = jnp.broadcast_to(scale, scale_out.shape)
    high, low, first, second = (column[:, depth + i].astype(jnp.float32) for i in range(4))
    new_master = advance(scale[None], grad[...], high + low, first, second)[1]
    block = new_master.astype(jnp.bfloat16)
    for peer in range(out.shape[0]):
        out[peer] = block


def place(core, source, *refs):
    out, sems = refs[-2:]
    copies = [
        pltpu.make_async_copy(source.at[:, z], out.at[z, :, core[0]], sems.at[z])
        for z in range(out.shape[0])
    ]
    for copy in copies:
        copy.start()
    for copy in copies:
        copy.wait()


SMEM = pl.BlockSpec(memory_space=pltpu.SMEM)
ANY = pl.BlockSpec(memory_space=pl.ANY)


def local(kernel, out_shape, count, out_specs=VMEM, scratch=()):
    return pl.pallas_call(
        kernel,
        out_shape=out_shape,
        in_specs=[VMEM] * count,
        out_specs=out_specs,
        scratch_shapes=list(scratch),
        compiler_params=pltpu.CompilerParams(vmem_limit_bytes=LIMIT),
        name=kernel.__name__,
    )


def put_half(core, half, whole=None):
    peers, depth, *tile = half.shape
    size = half.size * half.dtype.itemsize
    return pl.pallas_call(
        place,
        out_shape=jax.ShapeDtypeStruct((depth, peers, 2, *tile), half.dtype),
        in_specs=[SMEM, VMEM] + [ANY] * (whole is not None),
        out_specs=ANY,
        scratch_shapes=[pltpu.SemaphoreType.DMA((depth,))],
        input_output_aliases={2: 0} if whole is not None else {},
        compiler_params=pltpu.CompilerParams(vmem_limit_bytes=LIMIT),
        cost_estimate=pl.CostEstimate(flops=0, transcendentals=0, bytes_accessed=2 * size),
        name="put_half",
    )(core, half, *(() if whole is None else (whole,)))


def exchange(value, axes):
    return lax.all_to_all(value, axes, 0, 0, tiled=False)


def to_rows(shard):
    taps = shard.shape[0]
    return shard.reshape(taps, -1, LANES).transpose(1, 0, 2).reshape(-1, LANES)


def from_rows(rows, taps):
    return rows.reshape(-1, taps, LANES).transpose(1, 0, 2).reshape(taps, -1)


def body(
    inputs, weights, ln_gain, ln_bias, projection, targets, master, first_moment, second_moment
):
    depth, plane = lax.axis_size("z"), lax.axis_size(PLANE)
    taps, width = weights.shape[0], ln_gain.shape[0]
    tile = (taps * width // LANES, LANES)
    f32, bf16 = jnp.float32, jnp.bfloat16
    shape = jax.ShapeDtypeStruct
    windows, dpre, input_grad = local_pass(inputs, weights, ln_gain, ln_bias, projection, targets)
    term = jnp.einsum("bfo,bfki->koi", dpre, windows, preferred_element_type=f32).astype(bf16)
    term = term.reshape(taps, depth, plane, width).transpose(2, 0, 1, 3)
    term = lax.optimization_barrier(term).reshape(plane // 2, 2, taps, depth, width)
    core = lax.axis_index("core").reshape(1)
    away = lax.dynamic_index_in_dim(term, 1 - core[0], 1, keepdims=False)
    recv = lax.ppermute(away, "core", SWAP)
    recv, input_grad = lax.optimization_barrier((recv, input_grad))
    term = pl.pallas_call(
        merge,
        out_shape=shape(away.shape, bf16),
        in_specs=[SMEM, VMEM, VMEM],
        out_specs=VMEM,
        compiler_params=pltpu.CompilerParams(vmem_limit_bytes=LIMIT),
        name="merge",
    )(core, term, recv)
    shards = [to_rows(value) for value in (master, first_moment, second_moment)]
    packed = local(
        plane_sum, shape((depth + 4,) + tile, bf16), 4, VMEM, (pltpu.VMEM((depth,) + tile, f32),)
    )(exchange(term, PLANE[:2]), *shards)
    column = lax.all_gather(packed, "z")
    grad, piece = local(
        column_sum,
        (shape((depth,) + tile, f32), shape((plane, 8, LANES), f32)),
        1,
        (VMEM, VMEM),
    )(column)
    rows, scale = local(
        plane_update,
        (shape((plane // 2, depth) + tile, bf16), shape((8, LANES), f32)),
        3,
        (VMEM, VMEM),
    )(exchange(piece, PLANE), grad, column)
    grad = lax.dynamic_index_in_dim(grad, lax.axis_index("z"), 0, keepdims=False)
    fresh = [from_rows(value, taps) for value in advance(scale, grad, *shards)]
    update, new_master, new_first, new_second = fresh
    own = exchange(rows, PLANE[:2])
    other = lax.ppermute(own, "core", SWAP)
    whole = put_half(core, own)
    whole = put_half(1 - core, other, whole)
    new_weights = from_rows(whole, taps)
    return (input_grad, update, new_master, new_first, new_second, new_weights)


def solution(mesh):
    grid = Mesh(mesh.devices.reshape(16, 4, 4, 2), AXES)
    return jax.shard_map(
        body,
        mesh=grid,
        in_specs=(
            P(AXES, None, None),
            P(),
            P(),
            P(),
            P(),
            P(AXES, None),
            P(None, AXES),
            P(None, AXES),
            P(None, AXES),
        ),
        out_specs=(
            P(AXES, None, None),
            P(None, AXES),
            P(None, AXES),
            P(None, AXES),
            P(None, AXES),
            P(),
        ),
        check_vma=False,
    )
```
